512 devices in a mesh: ctx: 32 (over z, x_hi, core), head: 16 (over y, x_lo).
Axes of the slice: x: 4 (x_hi: 2, x_lo: 2; x = x_hi * 2 + x_lo), y: 8, z: 8, core: 2. Of those that a mesh axis runs over, the one named last changes fastest.
Arguments:
- tokens: bfloat16 [131072, 1024], P(('ctx', 'head')), may hold values from -11 to 11
- ln_gain: float32 [1024], replicated, may hold values from 0.1 to 1.9
- ln_bias: float32 [1024], replicated, may hold values from -3 to 3
- qkv_weight: bfloat16 [1024, 16, 192], P(None, 'head'), may hold values from -7 to 7
- out_weight: bfloat16 [1024, 1024], P('head'), may hold values from -0.75 to 0.75
- output_bias_vector: float32 [1024], replicated, may hold values from -3 to 3
- lengths: int32 [1024], replicated, may hold values from 1 to 512, 131072 in all
- pairs_dev: int32 [1024, 3], replicated, may hold values from 0 to 31, all different within a row; in each aligned block of 32 rows (0 to 31, 32 to 63, ...) at most 4 rows name the same one
- pairs_off: int32 [1024, 3], replicated, may hold values from 0 to 31
Outputs:
- attended_out: bfloat16 [131072, 1024], P(('ctx', 'head'))
The draws below stay inside these ranges and needn't reach their ends.
Inputs may be any that keep to these rules, and one draw needn't show every extreme that they name: The lengths sum to 131072. `pairs_dev`: each row names 3 different ctx indices; within the rows of one ctx index's 32 query blocks no ctx index is named more than 4 times.
All inputs are finite; a program needn't handle non-finite values.
Results may differ from the reference program's by a relative error of at most 0.0065.
The reference program's roundings to bfloat16 on the way count: a program that leaves them out, or rounds other values in their place, can miss the bound.
Values may be sent and summed in bfloat16 or wider, within the bound.
No kernel may reach another device: no remote copies, remote signals or barrier semaphores. Data moves between devices by JAX's collectives and lax.ppermute only.
A program may use at most 64 MiB of HBM per device.

```python
import math
import jax
import jax.numpy as jnp
import numpy as np
from jax import lax

D = 1024
HEADS = 16
HD = 64
BLK = 128
RAND = 3
LINE_MOST = 512
TOKENS = 131072
QB_DEV = 32
QBLOCKS = 1024
CAP = 4
LINES = 1024
N_CTX = 32


def draw_tokens(key, part):
    base_key = jax.random.fold_in(jax.random.fold_in(key, 17), 0)
    result = jnp.clip(jax.random.normal(base_key, (TOKENS, D), jnp.float32), -6.0, 6.0)
    return result.astype(jnp.bfloat16)


def draw_qkv_weight(key, part):
    raw_draw = jnp.clip(jax.random.normal(jax.random.fold_in(key, 29), (D, HEADS, 3 * HD), jnp.float32), -6.0, 6.0) / math.sqrt(D)
    result = raw_draw
    return result.astype(jnp.bfloat16)


def touch_ends(values, own_key, least, top_value):
    longest = values.shape.index(max(values.shape))
    spots = []
    for shift in (0, 1):
        where = [jax.random.randint(jax.random.fold_in(own_key, axis), (), 0, length) for axis, length in enumerate(values.shape)]
        where[longest] = (where[longest] + shift) % values.shape[longest]
        spots.append(tuple(where))
    return values.at[spots[0]].set(least).at[spots[1]].set(top_value)


def level_of(rng, extent, cuts, low, largest):
    factor_of, own = 1.0, jax.random.fold_in(rng, 6)
    for axis_at, blocks in cuts:
        draws = jnp.exp(jax.random.uniform(jax.random.fold_in(own, axis_at), (blocks,), jnp.float32, low / len(cuts), largest / len(cuts)))
        factor_of = factor_of * jnp.repeat(draws, extent[axis_at] // blocks).reshape([-1 if axis == axis_at else 1 for axis in range(len(extent))])
    return factor_of


def profile(amount, total, reach, lean):
    weights = [(1 << 20) // math.isqrt(rank ** lean) + 1 for rank in range(2, amount + 1)]
    spare, holding = total - reach - (amount - 1), [1] * (amount - 1)
    while spare > 0:
        free = [i for i in range(amount - 1) if holding[i] < reach]
        mass, left = sum([weights[i] for i in free]), spare
        for i in free:
            addition = min(reach - holding[i], max(1, left * weights[i] // mass), spare)
            holding[i] = holding[i] + addition
            spare = spare - addition
    return np.array([reach] + holding)


def uneven(key, count, total, most, slope):
    if count == 2:
        one = jax.random.randint(key, (), max(1, total - most), min(most, total - 1) + 1)
        return jnp.stack([one, total - one])
    sizes = jnp.asarray(profile(count, total, most, slope), jnp.int32)
    pairs = (count - 1) // 2
    giver, sink = sizes[1:1 + 2 * pairs:2], sizes[2:2 + 2 * pairs:2]
    slack = jnp.minimum(giver - 1, most - sink)
    passed = jax.random.randint(jax.random.fold_in(key, 1), (pairs,), 0, 1 << 20) % (slack + 1)
    sizes = sizes.at[1:1 + 2 * pairs:2].set(giver - passed).at[2:2 + 2 * pairs:2].set(sink + passed)
    return sizes[jax.random.permutation(jax.random.fold_in(key, 2), count)]


def assign_block(rng, own, number, rows, count, top, reach, slope):
    sequence = jax.random.permutation(rng, count)
    packed, usual = shares(count, rows * top, reach, slope, True), shares(count, rows * top, reach, slope, False)
    places = jnp.arange(count)

    def named(sizes, turn):
        used = int((sizes > 0).sum())
        fixed = max(1, used // 4)
        passed = fixed + (places - fixed + turn * (used - fixed)) % max(1, count - fixed)
        return jnp.zeros((count,), jnp.int32).at[sequence[jnp.where(places < fixed, places, passed)]].set(jnp.asarray(sizes, jnp.int32))

    sizes = jnp.where(number % 4 == 0, named(packed, number // 4), named(usual, number - number // 4 - 1))
    mixed = jax.random.permutation(jax.random.fold_in(own, 3), count)
    giver, receiver = mixed[0:count // 2 * 2:2], mixed[1:count // 2 * 2:2]
    margin = jnp.minimum(sizes[giver] - 1, reach - sizes[receiver]) // 2
    margin = jnp.where((giver == sequence[0]) | (receiver == sequence[0]) | (sizes[receiver] == 0), 0, jnp.maximum(margin, 0))
    passed = jax.random.randint(jax.random.fold_in(own, 4), (count // 2,), 0, 1 << 20) % (margin + 1)
    sizes = sizes.at[giver].add(-passed).at[receiver].add(passed)
    labels = jnp.searchsorted(jnp.cumsum(sizes), jnp.arange(rows * top), side="right").astype(jnp.int32)
    table = labels.reshape(top, rows).T
    table = table[jax.random.permutation(jax.random.fold_in(own, 1), rows)]
    turn = jax.random.randint(jax.random.fold_in(own, 2), (rows, 1), 0, top)
    return jnp.take_along_axis(table, (jnp.arange(top)[None, :] + turn) % top, axis=1)


def shares(count, total, reach, skew, full):
    loads = [(1 << 20) // math.isqrt(rank ** skew) + 1 for rank in range(1, count + 1)]
    largest = reach if full else min(reach, max(-(-total // count), total * loads[0] // sum(loads)))
    least = 1 if total - largest >= count - 1 else 0
    holding, spare = [largest] + [least] * (count - 1), total - largest - least * (count - 1)
    while spare > 0:
        movable = [i for i in range(1, count) if holding[i] < largest] or [i for i in range(1, count) if holding[i] < reach]
        whole, budget = sum([loads[i] for i in movable]), spare
        for i in movable:
            addition = min(reach - holding[i], max(1, budget * loads[i] // whole), spare)
            holding[i] = holding[i] + addition
            spare = spare - addition
    return np.array(holding)


def normal_values(key, shape, deviation, most, shards=(), kind=jnp.bfloat16):
    entries = jax.random.normal(key, shape, jnp.float32) * deviation
    if len(shards) > 0:
        entries = level_of(key, shape, shards, -0.22, 0.18) * entries
    return jnp.clip(entries, min=-most, max=most).astype(kind)


def setup_inputs(seed: int = 0) -> dict:
    key_list = jax.random.split(jax.random.key(seed), 10)
    tokens = draw_tokens(jax.random.fold_in(key_list[9], 71), 0)
    ln_gain = jnp.clip(1.0 + 0.18 * jax.random.normal(key_list[1], (D,), jnp.float32), 0.1, 1.9)
    ln_bias = normal_values(key_list[2], (D,), 0.5, 3.0, (), jnp.float32)
    qkv_weight = draw_qkv_weight(jax.random.fold_in(key_list[9], 71), 0)
    out_weight = normal_values(key_list[4], (D, D), HD ** -0.5, 0.75, ((0, 16),))
    output_bias_vector = normal_values(key_list[5], (D,), 0.5, 3.0, (), jnp.float32)
    lengths = uneven(key_list[6], LINES, TOKENS, LINE_MOST, 1).astype(jnp.int32)
    pairs_dev_keys = jax.random.split(jax.random.fold_in(key_list[7], 1), QBLOCKS // QB_DEV)
    pairs_dev_turns = jax.random.permutation(jax.random.fold_in(key_list[7], 3), QBLOCKS // QB_DEV)
    pairs_dev = jax.vmap(lambda own, number: assign_block(jax.random.fold_in(key_list[7], 2), own, number, QB_DEV, N_CTX, RAND, CAP, 2))(pairs_dev_keys, pairs_dev_turns).reshape((QBLOCKS, RAND))
    pairs_off = touch_ends(jax.random.randint(key_list[8], (QBLOCKS, RAND), 0, QB_DEV), jax.random.fold_in(key_list[8], 1), 0, QB_DEV - 1).astype(jnp.int32)
    return dict(tokens=tokens, ln_gain=ln_gain, ln_bias=ln_bias, qkv_weight=qkv_weight, out_weight=out_weight, output_bias_vector=output_bias_vector, lengths=lengths, pairs_dev=pairs_dev, pairs_off=pairs_off)


epsilon = 1e-05

def normalize(tokens, ln_gain, ln_bias):
    values = tokens.astype(jnp.float32)
    center = values - lax.optimization_barrier(jnp.mean(values, axis=-1, keepdims=True))
    spread = lax.optimization_barrier(jnp.mean(center * center, axis=-1, keepdims=True))
    return (center * lax.rsqrt(spread + epsilon) * ln_gain + ln_bias).astype(jnp.bfloat16)

def owning_line(line_end, positions):
    return jnp.searchsorted(line_end, positions, side='right').astype(jnp.int32)

def attend(queries, window_rows, window_line, query_line, global_kv, random_kv, head_dim):
    group_size = queries.shape[0]
    block_rows = queries.shape[1]
    windows = jnp.stack([window_rows[member * block_rows:(member + 3) * block_rows] for member in range(group_size)])
    window_ids = jnp.stack([window_line[member * block_rows:(member + 3) * block_rows] for member in range(group_size)])
    global_rows = jnp.broadcast_to(global_kv[None], (group_size,) + global_kv.shape)
    key_rows = jnp.concatenate([windows, global_rows, random_kv], axis=1)
    key_part = key_rows[..., :head_dim].astype(jnp.float32)
    value_part = key_rows[..., head_dim:].astype(jnp.float32)
    scores = jnp.einsum('gqhd,gkhd->ghqk', queries.astype(jnp.float32), key_part) * head_dim ** (-0.5)
    allowed_window = window_ids[:, None, :] == query_line[:, :, None]
    extra_keys = key_rows.shape[1] - 3 * block_rows
    allowed = jnp.concatenate([allowed_window, jnp.ones((group_size, block_rows, extra_keys), dtype=bool)], axis=2)
    scores = jnp.where(allowed[:, None], scores, -jnp.inf)
    row_max = lax.optimization_barrier(jnp.max(scores, axis=-1, keepdims=True))
    exp_scores = jnp.exp(scores - row_max)
    denominator = lax.optimization_barrier(jnp.sum(exp_scores, axis=-1))
    rounded = exp_scores.astype(jnp.bfloat16)
    summed = jnp.einsum('ghqk,gkhd->gqhd', rounded.astype(jnp.float32), value_part)
    return (summed / jnp.transpose(denominator, (0, 2, 1))[..., None]).astype(jnp.bfloat16)

def reference(tokens, ln_gain, ln_bias, qkv_weight, out_weight, output_bias_vector, lengths, pairs_dev, pairs_off):
    normed = normalize(tokens, ln_gain, ln_bias)
    projected_qkv = jnp.dot(normed, qkv_weight.reshape(D, HEADS * 3 * HD), preferred_element_type=jnp.float32)
    projected_qkv = projected_qkv.astype(jnp.bfloat16).reshape(TOKENS, HEADS, 3 * HD)
    q_blocks = projected_qkv[..., :HD].reshape(QBLOCKS, BLK, HEADS, HD)
    paired_key_value = projected_qkv[..., HD:]
    line_end = jnp.cumsum(lengths).astype(jnp.int32)
    positions = jnp.arange(-BLK, TOKENS + BLK, dtype=jnp.int32)
    inside = (positions >= 0) & (positions < TOKENS)
    ext_line = jnp.where(inside, owning_line(line_end, jnp.clip(positions, 0, TOKENS - 1)), -1).astype(jnp.int32)
    padded = jnp.pad(paired_key_value, ((BLK, BLK), (0, 0), (0, 0)))
    kv_blocks = paired_key_value.reshape(QBLOCKS, BLK, HEADS, 2 * HD)
    chosen = (pairs_dev * QB_DEV + pairs_off).astype(jnp.int32)
    global_kv = paired_key_value[:BLK]
    group_size = math.gcd(QBLOCKS, 4)

    def group_step(group_index):
        first_block = group_index * group_size
        window_rows = lax.dynamic_slice_in_dim(padded, first_block * BLK, (group_size + 2) * BLK, 0)
        window_line = lax.dynamic_slice_in_dim(ext_line, first_block * BLK, (group_size + 2) * BLK, 0)
        query_line = lax.dynamic_slice_in_dim(ext_line, (first_block + 1) * BLK, group_size * BLK, 0).reshape(group_size, BLK)
        queries = lax.dynamic_slice_in_dim(q_blocks, first_block, group_size, 0)
        picks = lax.dynamic_slice_in_dim(chosen, first_block, group_size, 0).reshape(-1)
        random_kv = jnp.take(kv_blocks, picks, axis=0).reshape(group_size, RAND * BLK, HEADS, 2 * HD)
        return attend(queries, window_rows, window_line, query_line, global_kv, random_kv, HD)
    attended = lax.map(group_step, jnp.arange(QBLOCKS // group_size, dtype=jnp.int32)).reshape(TOKENS, D)
    result = jnp.dot(attended, out_weight, preferred_element_type=jnp.float32) + output_bias_vector
    return result.astype(jnp.bfloat16)
```

```python
import jax
import jax.numpy as jnp
from jax import lax
from jax.experimental import pallas as pl
from jax.experimental.pallas import tpu as pltpu
from jax.sharding import PartitionSpec as P

BLK = 128
RAND = 3
CAP = 4
EPS = 1e-05
NEG = float("-inf")


def ln_kernel(tok_ref, gain_ref, bias_ref, norm_ref, normt_ref):
    values = tok_ref[...].astype(jnp.float32)
    center = values - jnp.mean(values, axis=-1, keepdims=True)
    spread = jnp.mean(center * center, axis=-1, keepdims=True)
    normed = center * lax.rsqrt(spread + EPS) * gain_ref[...] + bias_ref[...]
    norm_ref[...] = normed.astype(jnp.bfloat16)
    normt_ref[...] = jnp.transpose(normed).astype(jnp.bfloat16).reshape(normt_ref.shape)


def layer_norm(tokens, gain, bias, heads):
    rows, width = tokens.shape
    return pl.pallas_call(
        ln_kernel,
        out_shape=(
            jax.ShapeDtypeStruct((rows, width), jnp.bfloat16),
            jax.ShapeDtypeStruct((heads, width // heads, rows), jnp.bfloat16),
        ),
        name="layer_norm",
    )(tokens, gain.reshape(1, width), bias.reshape(1, width))


def pick_kernel(ids_ref, cells_ref, out_ref):
    def step(slot, carry):
        block = ids_ref[slot]
        cols = pl.ds(pl.multiple_of((block % 2) * BLK, BLK), BLK)
        out_ref[slot] = cells_ref[block // 2, :, cols]
        return carry

    lax.fori_loop(0, out_ref.shape[0], step, 0, unroll=4)


def pick_blocks(ids, cells):
    return pl.pallas_call(
        pick_kernel,
        out_shape=jax.ShapeDtypeStruct((ids.shape[0], cells.shape[1], BLK), jnp.bfloat16),
        in_specs=[
            pl.BlockSpec(memory_space=pltpu.SMEM),
            pl.BlockSpec(memory_space=pltpu.VMEM),
        ],
        out_specs=pl.BlockSpec(memory_space=pltpu.VMEM),
        name="pick_blocks",
    )(ids, cells)


def place_kernel(pos_ref, slots_ref, shared_ref, out_ref):
    per_dev = out_ref.shape[2] // BLK - 1

    def step(dev, carry):
        for j in range(per_dev):
            out_ref[dev, :, j * BLK : (j + 1) * BLK] = slots_ref[pos_ref[dev * per_dev + j]]
        out_ref[dev, :, per_dev * BLK :] = shared_ref[...]
        return carry

    lax.fori_loop(0, out_ref.shape[0], step, 0)


def place_blocks(pos, slots, shared, heads):
    per_dev = pos.shape[0] // heads
    return pl.pallas_call(
        place_kernel,
        out_shape=jax.ShapeDtypeStruct(
            (heads, slots.shape[1], (per_dev + 1) * BLK), jnp.bfloat16
        ),
        in_specs=[
            pl.BlockSpec(memory_space=pltpu.SMEM),
            pl.BlockSpec(memory_space=pltpu.VMEM),
            pl.BlockSpec(memory_space=pltpu.VMEM),
        ],
        out_specs=pl.BlockSpec(memory_space=pltpu.VMEM),
        name="place_blocks",
    )(pos, slots, shared)


def attend_kernel(q_ref, kl_ref, vl_ref, kr_ref, vr_ref, mask_ref, out_ref):
    lane = lax.broadcasted_iota(jnp.int32, (BLK, BLK), 1)
    first = lane < BLK // 2
    spread = RAND * BLK
    nt = (((1,), (1,)), ((), ()))
    f32 = jnp.float32
    for b in range(2):
        rows = slice(b * BLK, (b + 1) * BLK)
        near = slice(b * BLK, (b + 3) * BLK)
        far = slice(b * spread, (b + 1) * spread)
        shared = slice(2 * spread, 2 * spread + BLK)
        q_pair = q_ref[rows, :]
        parts = []
        for h in range(2):
            mine = first if h == 0 else jnp.logical_not(first)
            q = jnp.where(mine, q_pair, jnp.zeros_like(q_pair))
            s1 = jnp.dot(q, kl_ref[:, near], preferred_element_type=f32) + mask_ref[b]
            s2 = jnp.dot(q, kr_ref[:, far], preferred_element_type=f32)
            s3 = jnp.dot(q, kr_ref[:, shared], preferred_element_type=f32)
            top = jnp.maximum(
                jnp.max(jnp.maximum(s1, s2), axis=-1, keepdims=True),
                jnp.max(s3, axis=-1, keepdims=True),
            )
            p1 = jnp.exp(s1 - top)
            p2 = jnp.exp(s2 - top)
            p3 = jnp.exp(s3 - top)
            total = jnp.sum(p1 + p2, axis=-1, keepdims=True) + jnp.sum(
                p3, axis=-1, keepdims=True
            )
            acc = lax.dot_general(
                p1.astype(jnp.bfloat16), vl_ref[:, near], nt, preferred_element_type=f32
            )
            acc += lax.dot_general(
                p2.astype(jnp.bfloat16), vr_ref[:, far], nt, preferred_element_type=f32
            )
            acc += lax.dot_general(
                p3.astype(jnp.bfloat16), vr_ref[:, shared], nt, preferred_element_type=f32
            )
            parts.append(acc / total)
        out_ref[rows, :] = jnp.where(first, parts[0], parts[1]).astype(jnp.bfloat16)


def attend(q, kv_near, kv_far, mask):
    rows, width = q.shape
    pairs = width // BLK
    near, far = kv_near.shape[1], kv_far.shape[1]
    return pl.pallas_call(
        attend_kernel,
        out_shape=jax.ShapeDtypeStruct((rows, width), jnp.bfloat16),
        grid=(pairs,),
        in_specs=[
            pl.BlockSpec((rows, BLK), lambda i: (0, i)),
            pl.BlockSpec((BLK, near), lambda i: (i, 0)),
            pl.BlockSpec((BLK, near), lambda i: (i + pairs, 0)),
            pl.BlockSpec((BLK, far), lambda i: (i, 0)),
            pl.BlockSpec((BLK, far), lambda i: (i + pairs, 0)),
            pl.BlockSpec(mask.shape, lambda i: (0, 0, 0)),
        ],
        out_specs=pl.BlockSpec((rows, BLK), lambda i: (0, i)),
        name="attend",
    )(q, kv_near, kv_near, kv_far, kv_far, mask)


def exchange_plan(pairs_dev, pairs_off, ctx_count, ctx_index, lower):
    pair_count = lower.shape[0]
    all_dev = pairs_dev.reshape(ctx_count, pair_count)
    all_off = pairs_off.reshape(ctx_count, pair_count)
    own = all_dev == ctx_index
    rank = jnp.sum((own[:, None, :] & lower[None]).astype(jnp.int32), axis=2)
    slot = jnp.arange(CAP, dtype=jnp.int32)
    chosen = own[:, None, :] & (rank[:, None, :] == slot[None, :, None])
    send = jnp.sum(jnp.where(chosen, all_off[:, None, :], 0), axis=2).reshape(-1)
    own_dev = lax.dynamic_index_in_dim(all_dev, ctx_index, 0, keepdims=False)
    earlier = (own_dev[:, None] == own_dev[None, :]) & lower
    take = own_dev * CAP + jnp.sum(earlier.astype(jnp.int32), axis=1)
    return send, take


def window_mask(lengths, first_pos, doc_tokens, rows):
    line_end = jnp.cumsum(lengths)
    positions = first_pos - BLK + jnp.arange(rows + 2 * BLK, dtype=jnp.int32)
    line = jnp.sum((line_end[None, :] <= positions[:, None]).astype(jnp.int32), axis=1)
    inside = (positions >= 0) & (positions < doc_tokens)
    line = jnp.where(inside, line, -1)
    masks = []
    for b in range(rows // BLK):
        keys = line[b * BLK : (b + 3) * BLK]
        queries = line[(b + 1) * BLK : (b + 2) * BLK]
        masks.append(jnp.where(queries[:, None] == keys[None, :], 0.0, NEG))
    return jnp.stack(masks).astype(jnp.float32)


def per_device(
    tokens, ln_gain, ln_bias, qkv_weight, out_weight, out_bias, lengths, pairs_dev, pairs_off
):
    ctx_count = lax.axis_size("ctx")
    heads = lax.axis_size("head")
    devices = ctx_count * heads
    ctx_index = lax.axis_index("ctx")
    head_index = lax.axis_index("head")
    rows, width = tokens.shape
    hd = width // heads

    wt = jnp.transpose(qkv_weight[:, 0, :])
    shard = jnp.concatenate([wt[hd : 2 * hd], wt[2 * hd :], wt[:hd], out_weight])
    shard = shard.reshape(4, hd, width)
    gathered = lax.all_gather(shard, "head", axis=1, tiled=True)

    normed, normed_t = layer_norm(tokens, ln_gain, ln_bias, heads)
    cells = lax.all_to_all(normed_t, "head", split_axis=0, concat_axis=0, tiled=True)

    both = ("ctx", "head")
    right = [(i, i + 1) for i in range(devices - 1)]
    left = [(i + 1, i) for i in range(devices - 1)]
    before = lax.ppermute(normed_t[:, :, rows - BLK :], both, right)
    after = lax.ppermute(normed_t[:, :, :BLK], both, left)
    near = jnp.concatenate([before, normed_t, after], axis=2).reshape(width, rows + 2 * BLK)

    pair_count = (heads * rows // BLK) * RAND
    order = jnp.arange(pair_count, dtype=jnp.int32)
    lower = order[None, :] < order[:, None]
    send, take = exchange_plan(pairs_dev, pairs_off, ctx_count, ctx_index, lower)
    outgoing = pick_blocks(send, cells).reshape(ctx_count, CAP * hd, BLK)
    slots = lax.all_to_all(outgoing, "ctx", split_axis=0, concat_axis=0, tiled=True)
    slots = slots.reshape(ctx_count * CAP, hd, BLK)

    shared = jnp.where(ctx_index == 0, cells[0, :, :BLK], 0).astype(jnp.bfloat16)
    reach = 1
    while reach < ctx_count:
        hop = [(i, i + reach) for i in range(reach)]
        shared = shared + lax.ppermute(shared, "ctx", hop)
        reach *= 2

    placed = place_blocks(take, slots, shared, heads)
    far = lax.all_to_all(placed, "head", split_axis=0, concat_axis=0, tiled=True)
    far = far.reshape(width, far.shape[2])

    mask = window_mask(
        lengths, (ctx_index * heads + head_index) * rows, devices * rows, rows
    )

    f32 = jnp.float32
    w_kv = gathered[:2].reshape(2 * width, width)
    w_q = gathered[2]
    q = lax.dot_general(normed, w_q, (((1,), (1,)), ((), ())), preferred_element_type=f32)
    q = (q.astype(jnp.bfloat16).astype(f32) * hd**-0.5).astype(jnp.bfloat16)
    kv_near = jnp.dot(w_kv, near, preferred_element_type=f32).astype(jnp.bfloat16)
    kv_far = jnp.dot(w_kv, far, preferred_element_type=f32).astype(jnp.bfloat16)
    attended = attend(q, kv_near, kv_far, mask)
    projected = jnp.dot(attended, gathered[3], preferred_element_type=f32)
    return (projected + out_bias).astype(jnp.bfloat16)


def solution(mesh):
    in_specs = (
        P(("ctx", "head"), None),
        P(),
        P(),
        P(None, "head", None),
        P("head", None),
        P(),
        P(),
        P(),
        P(),
    )
    return jax.shard_map(
        per_device,
        mesh=mesh,
        in_specs=in_specs,
        out_specs=P(("ctx", "head"), None),
        check_vma=False,
    )
```

```python
import jax
import jax.numpy as jnp
from jax import lax
from jax.experimental import pallas as pl
from jax.experimental.pallas import tpu as pltpu
from jax.sharding import PartitionSpec as P

BLK = 128
RAND = 3
CAP = 4
EPS = 1e-05
NEG = float("-inf")
NT = (((1,), (1,)), ((), ()))


def ln_kernel(tok_ref, gain_ref, bias_ref, norm_ref, normt_ref):
    values = tok_ref[...].astype(jnp.float32)
    center = values - jnp.mean(values, axis=-1, keepdims=True)
    spread = jnp.mean(center * center, axis=-1, keepdims=True)
    normed = center * lax.rsqrt(spread + EPS) * gain_ref[...] + bias_ref[...]
    norm_ref[...] = normed.astype(jnp.bfloat16)
    normt_ref[...] = jnp.transpose(normed).astype(jnp.bfloat16).reshape(normt_ref.shape)


def layer_norm(tokens, gain, bias, heads):
    rows, width = tokens.shape
    return pl.pallas_call(
        ln_kernel,
        out_shape=(
            jax.ShapeDtypeStruct((rows, width), jnp.bfloat16),
            jax.ShapeDtypeStruct((heads, width // heads, rows), jnp.bfloat16),
        ),
        name="layer_norm",
    )(tokens, gain.reshape(1, width), bias.reshape(1, width))


def pick_kernel(ids_ref, cells_ref, out_ref):
    def step(slot, carry):
        block = ids_ref[slot]
        cols = pl.ds(pl.multiple_of((block % 2) * BLK, BLK), BLK)
        out_ref[slot] = cells_ref[block // 2, :, cols]
        return carry

    lax.fori_loop(0, out_ref.shape[0], step, 0, unroll=4)


def pick_blocks(ids, cells):
    return pl.pallas_call(
        pick_kernel,
        out_shape=jax.ShapeDtypeStruct((ids.shape[0], cells.shape[1], BLK), jnp.bfloat16),
        in_specs=[
            pl.BlockSpec(memory_space=pltpu.SMEM),
            pl.BlockSpec(memory_space=pltpu.VMEM),
        ],
        out_specs=pl.BlockSpec(memory_space=pltpu.VMEM),
        name="pick_blocks",
    )(ids, cells)


def place_kernel(pos_ref, slots_ref, out_ref):
    per_dev = out_ref.shape[2] // BLK

    def step(dev, carry):
        for j in range(per_dev):
            out_ref[dev, :, j * BLK : (j + 1) * BLK] = slots_ref[pos_ref[dev * per_dev + j]]
        return carry

    lax.fori_loop(0, out_ref.shape[0], step, 0)


def place_blocks(pos, slots, heads):
    per_dev = pos.shape[0] // heads
    return pl.pallas_call(
        place_kernel,
        out_shape=jax.ShapeDtypeStruct((heads, slots.shape[1], per_dev * BLK), jnp.bfloat16),
        in_specs=[
            pl.BlockSpec(memory_space=pltpu.SMEM),
            pl.BlockSpec(memory_space=pltpu.VMEM),
        ],
        out_specs=pl.BlockSpec(memory_space=pltpu.VMEM),
        name="place_blocks",
    )(pos, slots)


def head_lanes():
    return lax.broadcasted_iota(jnp.int32, (BLK, BLK), 1) < BLK // 2


def near_kernel(q_ref, k_ref, v_ref, mask_ref, acc_ref, top_ref, sum_ref):
    first = head_lanes()
    f32 = jnp.float32
    shared = slice(4 * BLK, 5 * BLK)
    for b in range(2):
        rows = slice(b * BLK, (b + 1) * BLK)
        near = slice(b * BLK, (b + 3) * BLK)
        q_pair = q_ref[rows, :]
        accs, tops, sums = [], [], []
        for mine in (first, jnp.logical_not(first)):
            q = jnp.where(mine, q_pair, jnp.zeros_like(q_pair))
            s = jnp.dot(q, k_ref[:, near], preferred_element_type=f32) + mask_ref[b]
            g = jnp.dot(q, k_ref[:, shared], preferred_element_type=f32)
            top = jnp.maximum(
                jnp.max(s, axis=-1, keepdims=True), jnp.max(g, axis=-1, keepdims=True)
            )
            p = jnp.exp(s - top)
            pg = jnp.exp(g - top)
            sums.append(
                jnp.sum(p, axis=-1, keepdims=True) + jnp.sum(pg, axis=-1, keepdims=True)
            )
            tops.append(top)
            accs.append(
                lax.dot_general(
                    p.astype(jnp.bfloat16), v_ref[:, near], NT, preferred_element_type=f32
                )
                + lax.dot_general(
                    pg.astype(jnp.bfloat16), v_ref[:, shared], NT, preferred_element_type=f32
                )
            )
        acc_ref[rows, :] = jnp.where(first, accs[0], accs[1])
        top_ref[rows, :] = jnp.where(first, tops[0], tops[1])
        sum_ref[rows, :] = jnp.where(first, sums[0], sums[1])


def near_attention(q, k, v, mask):
    rows, width = q.shape
    keys = k.shape[1]
    square = pl.BlockSpec((rows, BLK), lambda i: (0, i))
    wide = pl.BlockSpec((BLK, keys), lambda i: (i, 0))
    part = jax.ShapeDtypeStruct((rows, width), jnp.float32)
    return pl.pallas_call(
        near_kernel,
        out_shape=(part, part, part),
        grid=(width // BLK,),
        in_specs=[square, wide, wide, pl.BlockSpec(mask.shape, lambda i: (0, 0, 0))],
        out_specs=(square, square, square),
        name="near_attention",
    )(q, k, v, mask)


def far_kernel(q_ref, k_ref, v_ref, acc_ref, top_ref, sum_ref, out_ref):
    first = head_lanes()
    f32 = jnp.float32
    spread = RAND * BLK
    for b in range(2):
        rows = slice(b * BLK, (b + 1) * BLK)
        far = slice(b * spread, (b + 1) * spread)
        q_pair = q_ref[rows, :]
        outs = []
        for h, mine in enumerate((first, jnp.logical_not(first))):
            q = jnp.where(mine, q_pair, jnp.zeros_like(q_pair))
            s2 = jnp.dot(q, k_ref[:, far], preferred_element_type=f32)
            lane = h * (BLK // 2)
            old_top = top_ref[rows, lane : lane + 1]
            top = jnp.maximum(jnp.max(s2, axis=-1, keepdims=True), old_top)
            p2 = jnp.exp(s2 - top)
            scale = jnp.exp(old_top - top)
            total = jnp.sum(p2, axis=-1, keepdims=True)
            total += sum_ref[rows, lane : lane + 1] * scale
            acc = lax.dot_general(
                p2.astype(jnp.bfloat16), v_ref[:, far], NT, preferred_element_type=f32
            )
            acc += acc_ref[rows, :] * scale
            outs.append(acc / total)
        out_ref[rows, :] = jnp.where(first, outs[0], outs[1]).astype(jnp.bfloat16)


def far_attention(q, k, v, parts):
    rows, width = q.shape
    keys = k.shape[1]
    square = pl.BlockSpec((rows, BLK), lambda i: (0, i))
    wide = pl.BlockSpec((BLK, keys), lambda i: (i, 0))
    return pl.pallas_call(
        far_kernel,
        out_shape=jax.ShapeDtypeStruct((rows, width), jnp.bfloat16),
        grid=(width // BLK,),
        in_specs=[square, wide, wide, square, square, square],
        out_specs=square,
        name="far_attention",
    )(q, k, v, *parts)


def run_copies(copies):
    for copy in copies:
        copy.start()
    for copy in copies:
        copy.wait()


def piece_kernel(core_ref, wt_ref, out_w_ref, piece_ref, sems):
    rows, cols = wt_ref.shape[0], piece_ref.shape[1]
    mine = pl.ds(pl.multiple_of(core_ref[0] * cols, cols), cols)
    run_copies(
        [
            pltpu.make_async_copy(wt_ref.at[:, mine], piece_ref.at[:rows], sems.at[0]),
            pltpu.make_async_copy(out_w_ref.at[:, mine], piece_ref.at[rows:], sems.at[1]),
        ]
    )


def any_specs(count):
    return [pl.BlockSpec(memory_space=pl.ANY)] * count


def own_piece(core, wt, out_w):
    rows = wt.shape[0] + out_w.shape[0]
    return pl.pallas_call(
        piece_kernel,
        out_shape=jax.ShapeDtypeStruct((rows, wt.shape[1] // 2), jnp.bfloat16),
        in_specs=[pl.BlockSpec(memory_space=pltpu.SMEM)] + any_specs(2),
        out_specs=pl.BlockSpec(memory_space=pl.ANY),
        scratch_shapes=[pltpu.SemaphoreType.DMA((2,))],
        name="own_piece",
    )(core, wt, out_w)


def join_kernel(*refs):
    parts, out_ref, sems = refs[:-2], refs[-2], refs[-1]
    copies, row = [], 0
    for n, part in enumerate(parts):
        into = out_ref.at[pl.ds(row, part.shape[0])]
        copies.append(pltpu.make_async_copy(part, into, sems.at[n]))
        row += part.shape[0]
    run_copies(copies)


def join(*parts):
    rows = sum(part.shape[0] for part in parts)
    return pl.pallas_call(
        join_kernel,
        out_shape=jax.ShapeDtypeStruct((rows,) + parts[0].shape[1:], jnp.bfloat16),
        in_specs=any_specs(len(parts)),
        out_specs=pl.BlockSpec(memory_space=pl.ANY),
        scratch_shapes=[pltpu.SemaphoreType.DMA((len(parts),))],
        name="join",
    )(*parts)


def assemble_kernel(core_ref, *refs):
    sems = refs[-1]
    outs, parts = refs[-5:-1], refs[:-5]
    hd, width = outs[0].shape[1], outs[0].shape[2]
    cols = width // 2
    half = len(parts) // 2
    copies = []
    for n, part in enumerate(parts):
        side = core_ref[0] if n < half else 1 - core_ref[0]
        into_cols = pl.ds(pl.multiple_of(side * cols, cols), cols)
        count = part.shape[0]
        into_heads = pl.ds((n % half) * count, count)
        for k, out in enumerate(outs):
            copies.append(
                pltpu.make_async_copy(
                    part.at[:, pl.ds(k * hd, hd)],
                    out.at[into_heads, :, into_cols],
                    sems.at[n * len(outs) + k],
                )
            )
    run_copies(copies)


def assemble(core, parts, heads):
    count, rows, cols = parts[0].shape
    hd = rows // 4
    one = jax.ShapeDtypeStruct((heads, hd, 2 * cols), jnp.bfloat16)
    return pl.pallas_call(
        assemble_kernel,
        out_shape=(one,) * 4,
        in_specs=[pl.BlockSpec(memory_space=pltpu.SMEM)] + any_specs(len(parts)),
        out_specs=tuple(any_specs(4)),
        scratch_shapes=[pltpu.SemaphoreType.DMA((4 * len(parts),))],
        name="assemble",
    )(core, *parts)


def tied(value, *others):
    return lax.optimization_barrier((value,) + others)[0]


def shift(value, by, heads):
    pairs = [(i, (i + by) % heads) for i in range(heads)]
    return lax.ppermute(value, "head", pairs)


def swap(value, bits, devices):
    return lax.ppermute(value, ("ctx", "head"), [(i, i ^ bits) for i in range(devices)])


def widen(value, holders, steps):
    for step in steps:
        hop = [(i, i + step) for i in holders]
        value = value + lax.ppermute(value, ("ctx", "head"), hop)
        holders = holders + [i + step for i in holders]
    return value, holders


def exchange_plan(pairs_dev, pairs_off, ctx_count, ctx_index, lower):
    pair_count = lower.shape[0]
    all_dev = pairs_dev.reshape(ctx_count, pair_count)
    all_off = pairs_off.reshape(ctx_count, pair_count)
    own = all_dev == ctx_index
    rank = jnp.sum((own[:, None, :] & lower[None]).astype(jnp.int32), axis=2)
    slot = jnp.arange(CAP, dtype=jnp.int32)
    chosen = own[:, None, :] & (rank[:, None, :] == slot[None, :, None])
    send = jnp.sum(jnp.where(chosen, all_off[:, None, :], 0), axis=2).reshape(-1)
    own_dev = lax.dynamic_index_in_dim(all_dev, ctx_index, 0, keepdims=False)
    earlier = (own_dev[:, None] == own_dev[None, :]) & lower
    take = own_dev * CAP + jnp.sum(earlier.astype(jnp.int32), axis=1)
    return send, take


def window_mask(lengths, first_pos, doc_tokens, rows):
    line_end = jnp.cumsum(lengths)
    positions = first_pos - BLK + jnp.arange(rows + 2 * BLK, dtype=jnp.int32)
    line = jnp.sum((line_end[None, :] <= positions[:, None]).astype(jnp.int32), axis=1)
    inside = (positions >= 0) & (positions < doc_tokens)
    line = jnp.where(inside, line, -1)
    masks = []
    for b in range(rows // BLK):
        keys = line[b * BLK : (b + 3) * BLK]
        queries = line[(b + 1) * BLK : (b + 2) * BLK]
        masks.append(jnp.where(queries[:, None] == keys[None, :], 0.0, NEG))
    return jnp.stack(masks).astype(jnp.float32)


def per_device(
    tokens, ln_gain, ln_bias, qkv_weight, out_weight, out_bias, lengths, pairs_dev, pairs_off
):
    ctx_count = lax.axis_size("ctx")
    heads = lax.axis_size("head")
    devices = ctx_count * heads
    ctx_index = lax.axis_index("ctx")
    head_index = lax.axis_index("head")
    rows, width = tokens.shape
    hd = width // heads

    wt = jnp.transpose(qkv_weight[:, 0, :])
    core = (ctx_index % 2).astype(jnp.int32).reshape(1)
    place = ctx_index * heads + head_index

    normed, normed_t = layer_norm(tokens, ln_gain, ln_bias, heads)
    cells = lax.all_to_all(normed_t, "head", split_axis=0, concat_axis=0, tiled=True)

    own = own_piece(core, wt, out_weight)
    u1, d1 = shift(own, 2, heads), shift(own, -2, heads)

    shared = jnp.where(place == 0, normed_t[:, :, :BLK], 0).astype(jnp.bfloat16)
    holders = [0]
    shared, holders = widen(shared, holders, [16 * heads, 8 * heads])

    both = ("ctx", "head")
    right = [(i, i + 1) for i in range(devices - 1)]
    left = [(i + 1, i) for i in range(devices - 1)]
    before = lax.ppermute(normed_t[:, :, rows - BLK :], both, right)
    after = lax.ppermute(normed_t[:, :, :BLK], both, left)

    pair_count = (heads * rows // BLK) * RAND
    order = jnp.arange(pair_count, dtype=jnp.int32)
    lower = order[None, :] < order[:, None]
    send, take = exchange_plan(pairs_dev, pairs_off, ctx_count, ctx_index, lower)
    outgoing = pick_blocks(tied(send, u1, d1, shared), cells)
    outgoing = outgoing.reshape(ctx_count, CAP * hd, BLK)
    slots = lax.all_to_all(outgoing, "ctx", split_axis=0, concat_axis=0, tiled=True)
    slots = slots.reshape(ctx_count * CAP, hd, BLK)

    mid = own.shape[0] // 2
    u2, d2 = shift(u1, 2, heads), shift(d1, -2, heads)
    u3, d3 = shift(u2, 2, heads), shift(d2, -2, heads)
    u4, d4 = shift(u3[:mid], 2, heads), shift(d3[mid:], -2, heads)
    shape = (heads // 4,) + own.shape
    a = join(own, u1, d1, u2).reshape(shape)
    b = join(d2, u3, d3, u4, d4).reshape(shape)
    c = swap(a, 1, devices)
    d = swap(b, 2 * heads + 1, devices)
    shared, holders = widen(shared, holders, [4 * heads, heads, 2 * heads, 8, 4, 2, 1])

    placed = place_blocks(tied(take, c, d, shared), slots, heads)
    far = lax.all_to_all(placed, "head", split_axis=0, concat_axis=0, tiled=True)
    far = far.reshape(width, far.shape[2])

    mine = [a, b, c, d]
    other = [swap(part, heads, devices) for part in mine]
    near = jnp.concatenate([before, normed_t, after, shared], axis=2)
    near = near.reshape(width, near.shape[2])

    mask = window_mask(lengths, place * rows, devices * rows, rows)

    f32 = jnp.float32
    bf16 = jnp.bfloat16
    w_q, w_k, w_v, w_o = (
        w.reshape(width, width)
        for w in assemble(core, mine + other, heads)
    )
    q = lax.dot_general(normed, w_q, NT, preferred_element_type=f32)
    q = (q.astype(bf16).astype(f32) * hd**-0.5).astype(bf16)
    k_near = jnp.dot(w_k, near, preferred_element_type=f32).astype(bf16)
    v_near = jnp.dot(w_v, near, preferred_element_type=f32).astype(bf16)
    parts = near_attention(q, k_near, v_near, mask)
    k_far = jnp.dot(w_k, far, preferred_element_type=f32).astype(bf16)
    v_far = jnp.dot(w_v, far, preferred_element_type=f32).astype(bf16)
    attended = far_attention(q, k_far, v_far, parts)
    projected = jnp.dot(attended, w_o, preferred_element_type=f32)
    return (projected + out_bias).astype(bf16)


def solution(mesh):
    in_specs = (
        P(("ctx", "head"), None),
        P(),
        P(),
        P(None, "head", None),
        P("head", None),
        P(),
        P(),
        P(),
        P(),
    )
    return jax.shard_map(
        per_device,
        mesh=mesh,
        in_specs=in_specs,
        out_specs=P(("ctx", "head"), None),
        check_vma=False,
    )
```

```python
import jax
import jax.numpy as jnp
from jax import lax
from jax.experimental import pallas as pl
from jax.experimental.pallas import tpu as pltpu
from jax.sharding import PartitionSpec as P

BLK = 128
RAND = 3
CAP = 4
EPS = 1e-05
NEG = float("-inf")
TN = (((0,), (1,)), ((), ()))


def ln_kernel(tok_ref, gain_ref, bias_ref, normt_ref):
    values = tok_ref[...].astype(jnp.float32)
    center = values - jnp.mean(values, axis=-1, keepdims=True)
    spread = jnp.mean(center * center, axis=-1, keepdims=True)
    normed = center * lax.rsqrt(spread + EPS) * gain_ref[...] + bias_ref[...]
    normt_ref[...] = jnp.transpose(normed).astype(jnp.bfloat16).reshape(normt_ref.shape)


def layer_norm(tokens, gain, bias, heads):
    rows, width = tokens.shape
    return pl.pallas_call(
        ln_kernel,
        out_shape=jax.ShapeDtypeStruct((heads, width // heads, rows), jnp.bfloat16),
        name="layer_norm",
    )(tokens, gain.reshape(1, width), bias.reshape(1, width))


def pick_kernel(ids_ref, cells_ref, out_ref):
    def step(slot, carry):
        block = ids_ref[slot]
        cols = pl.ds(pl.multiple_of((block % 2) * BLK, BLK), BLK)
        out_ref[slot] = cells_ref[block // 2, :, cols]
        return carry

    lax.fori_loop(0, out_ref.shape[0], step, 0, unroll=4)


def pick_blocks(ids, cells):
    return pl.pallas_call(
        pick_kernel,
        out_shape=jax.ShapeDtypeStruct((ids.shape[0], cells.shape[1], BLK), jnp.bfloat16),
        in_specs=[
            pl.BlockSpec(memory_space=pltpu.SMEM),
            pl.BlockSpec(memory_space=pltpu.VMEM),
        ],
        out_specs=pl.BlockSpec(memory_space=pltpu.VMEM),
        name="pick_blocks",
    )(ids, cells)


def place_kernel(pos_ref, slots_ref, out_ref):
    per_dev = out_ref.shape[2] // BLK

    def step(dev, carry):
        for j in range(per_dev):
            out_ref[dev, :, j * BLK : (j + 1) * BLK] = slots_ref[pos_ref[dev * per_dev + j]]
        return carry

    lax.fori_loop(0, out_ref.shape[0], step, 0)


def place_blocks(pos, slots, heads):
    per_dev = pos.shape[0] // heads
    return pl.pallas_call(
        place_kernel,
        out_shape=jax.ShapeDtypeStruct((heads, slots.shape[1], per_dev * BLK), jnp.bfloat16),
        in_specs=[
            pl.BlockSpec(memory_space=pltpu.SMEM),
            pl.BlockSpec(memory_space=pltpu.VMEM),
        ],
        out_specs=pl.BlockSpec(memory_space=pltpu.VMEM),
        name="place_blocks",
    )(pos, slots)


def both_heads(qt_pair):
    half = qt_pair.shape[0] // 2
    none = jnp.zeros((half, qt_pair.shape[1]), qt_pair.dtype)
    top = jnp.concatenate([qt_pair[:half], none], axis=1)
    return jnp.concatenate([top, jnp.concatenate([none, qt_pair[half:]], axis=1)], axis=0)


def own_halves(wide):
    half, cols = wide.shape[0] // 2, wide.shape[1] // 2
    return jnp.concatenate([wide[:half, :cols], wide[half:, cols:]], axis=0)


def spread_rows(row, half):
    cols = row.shape[1] // 2
    top = jnp.broadcast_to(row[:, :cols], (half, cols))
    return jnp.concatenate([top, jnp.broadcast_to(row[:, cols:], (half, cols))], axis=0)


def near_kernel(qt_ref, k_ref, vt_ref, mask_ref, acc_ref, top_ref, sum_ref):
    f32 = jnp.float32
    shared = slice(4 * BLK, 5 * BLK)
    for b in range(2):
        cols = slice(b * BLK, (b + 1) * BLK)
        near = slice(b * BLK, (b + 3) * BLK)
        q = both_heads(qt_ref[:, cols])
        mask = mask_ref[b]
        s = jnp.dot(k_ref[near, :], q, preferred_element_type=f32)
        s = s + jnp.concatenate([mask, mask], axis=1)
        g = jnp.dot(k_ref[shared, :], q, preferred_element_type=f32)
        top = jnp.maximum(jnp.max(s, axis=0, keepdims=True), jnp.max(g, axis=0, keepdims=True))
        p = jnp.exp(s - top)
        pg = jnp.exp(g - top)
        total = jnp.sum(p, axis=0, keepdims=True) + jnp.sum(pg, axis=0, keepdims=True)
        acc = jnp.dot(vt_ref[:, near], p.astype(jnp.bfloat16), preferred_element_type=f32)
        acc += jnp.dot(vt_ref[:, shared], pg.astype(jnp.bfloat16), preferred_element_type=f32)
        acc_ref[:, cols] = own_halves(acc)
        top_ref[0, b] = jnp.broadcast_to(top, top_ref.shape[2:])
        sum_ref[0, b] = jnp.broadcast_to(total, sum_ref.shape[2:])


def far_kernel(qt_ref, k_ref, vt_ref, acc_ref, top_ref, sum_ref, out_ref):
    f32 = jnp.float32
    spread = RAND * BLK
    for b in range(2):
        cols = slice(b * BLK, (b + 1) * BLK)
        far = slice(b * spread, (b + 1) * spread)
        q = both_heads(qt_ref[:, cols])
        s = jnp.dot(k_ref[far, :], q, preferred_element_type=f32)
        old_top = top_ref[0, b, :1]
        top = jnp.maximum(jnp.max(s, axis=0, keepdims=True), old_top)
        p = jnp.exp(s - top)
        scale = jnp.exp(old_top - top)
        total = jnp.sum(p, axis=0, keepdims=True) + sum_ref[0, b, :1] * scale
        acc = jnp.dot(vt_ref[:, far], p.astype(jnp.bfloat16), preferred_element_type=f32)
        half = acc.shape[0] // 2
        acc = own_halves(acc) + acc_ref[:, cols] * spread_rows(scale, half)
        out_ref[:, cols] = (acc / spread_rows(total, half)).astype(jnp.bfloat16)


def pair_specs(rows, keys):
    tall = pl.BlockSpec((BLK, rows), lambda i: (i, 0))
    k_spec = pl.BlockSpec((keys, BLK), lambda i: (0, i))
    vt_spec = pl.BlockSpec((BLK, keys), lambda i: (i, 0))
    row = pl.BlockSpec((1, rows // BLK, 8, 2 * BLK), lambda i: (i, 0, 0, 0))
    return tall, k_spec, vt_spec, row


def near_attention(qt, k, vt, mask):
    width, rows = qt.shape
    pairs = width // BLK
    tall, k_spec, vt_spec, row = pair_specs(rows, k.shape[0])
    stat = jax.ShapeDtypeStruct((pairs, rows // BLK, 8, 2 * BLK), jnp.float32)
    return pl.pallas_call(
        near_kernel,
        out_shape=(jax.ShapeDtypeStruct((width, rows), jnp.float32), stat, stat),
        grid=(pairs,),
        in_specs=[tall, k_spec, vt_spec, pl.BlockSpec(mask.shape, lambda i: (0, 0, 0))],
        out_specs=(tall, row, row),
        name="near_attention",
    )(qt, k, vt, mask)


def far_attention(qt, k, vt, parts):
    width, rows = qt.shape
    tall, k_spec, vt_spec, row = pair_specs(rows, k.shape[0])
    return pl.pallas_call(
        far_kernel,
        out_shape=jax.ShapeDtypeStruct((width, rows), jnp.bfloat16),
        grid=(width // BLK,),
        in_specs=[tall, k_spec, vt_spec, tall, row, row],
        out_specs=tall,
        name="far_attention",
    )(qt, k, vt, *parts)


def run_copies(copies):
    for copy in copies:
        copy.start()
    for copy in copies:
        copy.wait()


def piece_kernel(core_ref, wt_ref, out_w_ref, piece_ref, sems):
    rows, cols = wt_ref.shape[0], piece_ref.shape[1]
    mine = pl.ds(pl.multiple_of(core_ref[0] * cols, cols), cols)
    run_copies(
        [
            pltpu.make_async_copy(wt_ref.at[:, mine], piece_ref.at[:rows], sems.at[0]),
            pltpu.make_async_copy(out_w_ref.at[:, mine], piece_ref.at[rows:], sems.at[1]),
        ]
    )


def any_specs(count):
    return [pl.BlockSpec(memory_space=pl.ANY)] * count


def own_piece(core, wt, out_w):
    rows = wt.shape[0] + out_w.shape[0]
    return pl.pallas_call(
        piece_kernel,
        out_shape=jax.ShapeDtypeStruct((rows, wt.shape[1] // 2), jnp.bfloat16),
        in_specs=[pl.BlockSpec(memory_space=pltpu.SMEM)] + any_specs(2),
        out_specs=pl.BlockSpec(memory_space=pltpu.VMEM),
        scratch_shapes=[pltpu.SemaphoreType.DMA((2,))],
        name="own_piece",
    )(core, wt, out_w)


def join_kernel(*refs):
    parts, out_ref, sems = refs[:-2], refs[-2], refs[-1]
    copies, row = [], 0
    for n, part in enumerate(parts):
        into = out_ref.at[pl.ds(row, part.shape[0])]
        copies.append(pltpu.make_async_copy(part, into, sems.at[n]))
        row += part.shape[0]
    run_copies(copies)


def join(*parts):
    rows = sum(part.shape[0] for part in parts)
    return pl.pallas_call(
        join_kernel,
        out_shape=jax.ShapeDtypeStruct((rows,) + parts[0].shape[1:], jnp.bfloat16),
        in_specs=any_specs(len(parts)),
        out_specs=pl.BlockSpec(memory_space=pltpu.VMEM),
        scratch_shapes=[pltpu.SemaphoreType.DMA((len(parts),))],
        name="join",
    )(*parts)


def assemble_kernel(core_ref, *refs):
    sems = refs[-1]
    outs, parts = refs[-5:-1], refs[:-5]
    hd, width = outs[0].shape[1], outs[0].shape[2]
    cols = width // 2
    half = len(parts) // 2
    copies = []
    for n, part in enumerate(parts):
        side = core_ref[0] if n < half else 1 - core_ref[0]
        into_cols = pl.ds(pl.multiple_of(side * cols, cols), cols)
        count = part.shape[0]
        into_heads = pl.ds((n % half) * count, count)
        for k, out in enumerate(outs):
            copies.append(
                pltpu.make_async_copy(
                    part.at[:, pl.ds(k * hd, hd)],
                    out.at[into_heads, :, into_cols],
                    sems.at[n * len(outs) + k],
                )
            )
    run_copies(copies)


def assemble(core, parts, heads):
    count, rows, cols = parts[0].shape
    hd = rows // 4
    one = jax.ShapeDtypeStruct((heads, hd, 2 * cols), jnp.bfloat16)
    return pl.pallas_call(
        assemble_kernel,
        out_shape=(one,) * 4,
        in_specs=[pl.BlockSpec(memory_space=pltpu.SMEM)] + any_specs(len(parts)),
        out_specs=(pl.BlockSpec(memory_space=pltpu.VMEM),) * 4,
        scratch_shapes=[pltpu.SemaphoreType.DMA((4 * len(parts),))],
        name="assemble",
    )(core, *parts)


def tied(value, *others):
    return lax.optimization_barrier((value,) + others)[0]


def shift(value, by, heads):
    pairs = [(i, (i + by) % heads) for i in range(heads)]
    return lax.ppermute(value, "head", pairs)


def swap(value, bits, devices):
    return lax.ppermute(value, ("ctx", "head"), [(i, i ^ bits) for i in range(devices)])


def widen(value, holders, steps):
    for step in steps:
        hop = [(i, i + step) for i in holders]
        value = value + lax.ppermute(value, ("ctx", "head"), hop)
        holders = holders + [i + step for i in holders]
    return value, holders


def exchange_plan(pairs_dev, pairs_off, ctx_count, ctx_index, lower):
    pair_count = lower.shape[0]
    all_dev = pairs_dev.reshape(ctx_count, pair_count)
    all_off = pairs_off.reshape(ctx_count, pair_count)
    own = all_dev == ctx_index
    rank = jnp.sum((own[:, None, :] & lower[None]).astype(jnp.int32), axis=2)
    slot = jnp.arange(CAP, dtype=jnp.int32)
    chosen = own[:, None, :] & (rank[:, None, :] == slot[None, :, None])
    send = jnp.sum(jnp.where(chosen, all_off[:, None, :], 0), axis=2).reshape(-1)
    own_dev = lax.dynamic_index_in_dim(all_dev, ctx_index, 0, keepdims=False)
    earlier = (own_dev[:, None] == own_dev[None, :]) & lower
    take = own_dev * CAP + jnp.sum(earlier.astype(jnp.int32), axis=1)
    return send, take


def window_mask(lengths, first_pos, doc_tokens, rows):
    line_end = jnp.cumsum(lengths)
    positions = first_pos - BLK + jnp.arange(rows + 2 * BLK, dtype=jnp.int32)
    line = jnp.sum((line_end[None, :] <= positions[:, None]).astype(jnp.int32), axis=1)
    inside = (positions >= 0) & (positions < doc_tokens)
    line = jnp.where(inside, line, -1)
    masks = []
    for b in range(rows // BLK):
        keys = line[b * BLK : (b + 3) * BLK]
        queries = line[(b + 1) * BLK : (b + 2) * BLK]
        masks.append(jnp.where(keys[:, None] == queries[None, :], 0.0, NEG))
    return jnp.stack(masks).astype(jnp.float32)


def per_device(
    tokens, ln_gain, ln_bias, qkv_weight, out_weight, out_bias, lengths, pairs_dev, pairs_off
):
    ctx_count = lax.axis_size("ctx")
    heads = lax.axis_size("head")
    devices = ctx_count * heads
    ctx_index = lax.axis_index("ctx")
    head_index = lax.axis_index("head")
    rows, width = tokens.shape
    hd = width // heads

    wt = jnp.transpose(qkv_weight[:, 0, :])
    core = (ctx_index % 2).astype(jnp.int32).reshape(1)
    place = ctx_index * heads + head_index

    normed_t = layer_norm(tokens, ln_gain, ln_bias, heads)
    cells = lax.all_to_all(normed_t, "head", split_axis=0, concat_axis=0, tiled=True)

    own = own_piece(core, wt, out_weight)
    u1, d1 = shift(own, 2, heads), shift(own, -2, heads)

    shared = jnp.where(place == 0, normed_t[:, :, :BLK], 0).astype(jnp.bfloat16)
    holders = [0]
    shared, holders = widen(shared, holders, [16 * heads, 8 * heads, 4 * heads])

    both = ("ctx", "head")
    right = [(i, i + 1) for i in range(devices - 1)]
    left = [(i + 1, i) for i in range(devices - 1)]
    before = lax.ppermute(normed_t[:, :, rows - BLK :], both, right)
    after = lax.ppermute(normed_t[:, :, :BLK], both, left)

    pair_count = (heads * rows // BLK) * RAND
    order = jnp.arange(pair_count, dtype=jnp.int32)
    lower = order[None, :] < order[:, None]
    send, take = exchange_plan(pairs_dev, pairs_off, ctx_count, ctx_index, lower)
    outgoing = pick_blocks(tied(send, u1, d1, shared), cells)
    outgoing = outgoing.reshape(ctx_count, CAP * hd, BLK)
    slots = lax.all_to_all(outgoing, "ctx", split_axis=0, concat_axis=0, tiled=True)
    slots = slots.reshape(ctx_count * CAP, hd, BLK)

    mid = own.shape[0] // 2
    u2, d2 = shift(u1, 2, heads), shift(d1, -2, heads)
    u3, d3 = shift(u2, 2, heads), shift(d2, -2, heads)
    u4, d4 = shift(u3[:mid], 2, heads), shift(d3[mid:], -2, heads)
    shape = (heads // 4,) + own.shape
    a = join(own, u1, d1, u2).reshape(shape)
    b = join(d2, u3, d3, u4, d4).reshape(shape)
    c = swap(a, 1, devices)
    d = swap(b, 2 * heads + 1, devices)
    shared, holders = widen(shared, holders, [heads, 2 * heads, 8, 4, 2, 1])

    placed = place_blocks(tied(take, c, d, shared, before, after), slots, heads)
    far = lax.all_to_all(placed, "head", split_axis=0, concat_axis=0, tiled=True)
    far = far.reshape(width, far.shape[2])

    mine = [a, b, c, d]
    other = [swap(part, heads, devices) for part in mine]
    near = jnp.concatenate([before, normed_t, after, shared], axis=2)
    near = near.reshape(width, near.shape[2])

    mask = window_mask(lengths, place * rows, devices * rows, rows)

    f32 = jnp.float32
    bf16 = jnp.bfloat16
    weights = assemble(core, mine + other, heads)
    w_q, w_k, w_v, w_o = (w.reshape(width, width) for w in weights)
    own_t = normed_t.reshape(width, rows)
    qt = jnp.dot(w_q, own_t, preferred_element_type=f32).astype(bf16)
    qt = (qt.astype(f32) * hd**-0.5).astype(bf16)
    k_near = lax.dot_general(near, w_k, TN, preferred_element_type=f32).astype(bf16)
    vt_near = jnp.dot(w_v, near, preferred_element_type=f32).astype(bf16)
    parts = near_attention(qt, k_near, vt_near, mask)
    k_far = lax.dot_general(far, w_k, TN, preferred_element_type=f32).astype(bf16)
    vt_far = jnp.dot(w_v, far, preferred_element_type=f32).astype(bf16)
    attended = far_attention(qt, k_far, vt_far, parts)
    projected = lax.dot_general(
        attended, w_o, (((0,), (0,)), ((), ())), preferred_element_type=f32
    )
    return (projected + out_bias).astype(bf16)


def solution(mesh):
    in_specs = (
        P(("ctx", "head"), None),
        P(),
        P(),
        P(None, "head", None),
        P("head", None),
        P(),
        P(),
        P(),
        P(),
    )
    return jax.shard_map(
        per_device,
        mesh=mesh,
        in_specs=in_specs,
        out_specs=P(("ctx", "head"), None),
        check_vma=False,
    )
```

```python
import jax
import jax.numpy as jnp
from jax import lax
from jax.experimental import pallas as pl
from jax.experimental.pallas import tpu as pltpu
from jax.sharding import PartitionSpec as P

BLK = 128
RAND = 3
CAP = 4
SLOTS = CAP + 1
EPS = 1e-05
NEG = float("-inf")
TN = (((0,), (1,)), ((), ()))


def ln_kernel(tok_ref, gain_ref, bias_ref, normt_ref):
    values = tok_ref[...].astype(jnp.float32)
    center = values - jnp.mean(values, axis=-1, keepdims=True)
    spread = jnp.mean(center * center, axis=-1, keepdims=True)
    normed = center * lax.rsqrt(spread + EPS) * gain_ref[...] + bias_ref[...]
    normt_ref[...] = jnp.transpose(normed).astype(jnp.bfloat16).reshape(normt_ref.shape)


def layer_norm(tokens, gain, bias, heads):
    rows, width = tokens.shape
    return pl.pallas_call(
        ln_kernel,
        out_shape=jax.ShapeDtypeStruct((heads, width // heads, rows), jnp.bfloat16),
        name="layer_norm",
    )(tokens, gain.reshape(1, width), bias.reshape(1, width))


def pick_kernel(ids_ref, cells_ref, out_ref):
    def step(slot, carry):
        block = ids_ref[slot]
        cols = pl.ds(pl.multiple_of((block % 2) * BLK, BLK), BLK)
        out_ref[slot] = cells_ref[block // 2, :, cols]
        return carry

    lax.fori_loop(0, out_ref.shape[0], step, 0, unroll=4)


def pick_blocks(ids, cells):
    return pl.pallas_call(
        pick_kernel,
        out_shape=jax.ShapeDtypeStruct((ids.shape[0], cells.shape[1], BLK), jnp.bfloat16),
        in_specs=[
            pl.BlockSpec(memory_space=pltpu.SMEM),
            pl.BlockSpec(memory_space=pltpu.VMEM),
        ],
        out_specs=pl.BlockSpec(memory_space=pltpu.VMEM),
        name="pick_blocks",
    )(ids, cells)


def place_kernel(pos_ref, slots_ref, out_ref):
    per_dev = out_ref.shape[2] // BLK

    def step(dev, carry):
        for j in range(per_dev):
            out_ref[dev, :, j * BLK : (j + 1) * BLK] = slots_ref[pos_ref[dev * per_dev + j]]
        return carry

    lax.fori_loop(0, out_ref.shape[0], step, 0)


def place_blocks(pos, slots, heads):
    per_dev = pos.shape[0] // heads
    return pl.pallas_call(
        place_kernel,
        out_shape=jax.ShapeDtypeStruct((heads, slots.shape[1], per_dev * BLK), jnp.bfloat16),
        in_specs=[
            pl.BlockSpec(memory_space=pltpu.SMEM),
            pl.BlockSpec(memory_space=pltpu.VMEM),
        ],
        out_specs=pl.BlockSpec(memory_space=pltpu.VMEM),
        name="place_blocks",
    )(pos, slots)


def both_heads(qt_pair):
    half = qt_pair.shape[0] // 2
    none = jnp.zeros((half, qt_pair.shape[1]), qt_pair.dtype)
    top = jnp.concatenate([qt_pair[:half], none], axis=1)
    return jnp.concatenate([top, jnp.concatenate([none, qt_pair[half:]], axis=1)], axis=0)


def own_halves(wide):
    half, cols = wide.shape[0] // 2, wide.shape[1] // 2
    return jnp.concatenate([wide[:half, :cols], wide[half:, cols:]], axis=0)


def spread_rows(row, half):
    cols = row.shape[1] // 2
    top = jnp.broadcast_to(row[:, :cols], (half, cols))
    return jnp.concatenate([top, jnp.broadcast_to(row[:, cols:], (half, cols))], axis=0)


def near_kernel(qt_ref, k_ref, vt_ref, mask_ref, acc_ref, top_ref, sum_ref):
    f32 = jnp.float32
    for b in range(2):
        cols = slice(b * BLK, (b + 1) * BLK)
        near = slice(b * BLK, (b + 3) * BLK)
        q = both_heads(qt_ref[:, cols])
        mask = mask_ref[b]
        s = jnp.dot(k_ref[near, :], q, preferred_element_type=f32)
        s = s + jnp.concatenate([mask, mask], axis=1)
        top = jnp.max(s, axis=0, keepdims=True)
        p = jnp.exp(s - top)
        total = jnp.sum(p, axis=0, keepdims=True)
        acc = jnp.dot(vt_ref[:, near], p.astype(jnp.bfloat16), preferred_element_type=f32)
        acc_ref[:, cols] = own_halves(acc)
        top_ref[0, b] = jnp.broadcast_to(top, top_ref.shape[2:])
        sum_ref[0, b] = jnp.broadcast_to(total, sum_ref.shape[2:])


def far_kernel(qt_ref, k_ref, vt_ref, acc_ref, top_ref, sum_ref, out_ref):
    f32 = jnp.float32
    spread = RAND * BLK
    shared = slice(2 * spread, 2 * spread + BLK)
    for b in range(2):
        cols = slice(b * BLK, (b + 1) * BLK)
        far = slice(b * spread, (b + 1) * spread)
        q = both_heads(qt_ref[:, cols])
        s = jnp.dot(k_ref[far, :], q, preferred_element_type=f32)
        g = jnp.dot(k_ref[shared, :], q, preferred_element_type=f32)
        old_top = top_ref[0, b, :1]
        top = jnp.maximum(jnp.max(s, axis=0, keepdims=True), old_top)
        top = jnp.maximum(jnp.max(g, axis=0, keepdims=True), top)
        p = jnp.exp(s - top)
        pg = jnp.exp(g - top)
        scale = jnp.exp(old_top - top)
        total = jnp.sum(p, axis=0, keepdims=True) + sum_ref[0, b, :1] * scale
        total += jnp.sum(pg, axis=0, keepdims=True)
        acc = jnp.dot(vt_ref[:, far], p.astype(jnp.bfloat16), preferred_element_type=f32)
        acc += jnp.dot(vt_ref[:, shared], pg.astype(jnp.bfloat16), preferred_element_type=f32)
        half = acc.shape[0] // 2
        acc = own_halves(acc) + acc_ref[:, cols] * spread_rows(scale, half)
        out_ref[:, cols] = (acc / spread_rows(total, half)).astype(jnp.bfloat16)


def pair_specs(rows, keys):
    tall = pl.BlockSpec((BLK, rows), lambda i: (i, 0))
    k_spec = pl.BlockSpec((keys, BLK), lambda i: (0, i))
    vt_spec = pl.BlockSpec((BLK, keys), lambda i: (i, 0))
    row = pl.BlockSpec((1, rows // BLK, 8, 2 * BLK), lambda i: (i, 0, 0, 0))
    return tall, k_spec, vt_spec, row


def near_attention(qt, k, vt, mask):
    width, rows = qt.shape
    pairs = width // BLK
    tall, k_spec, vt_spec, row = pair_specs(rows, k.shape[0])
    stat = jax.ShapeDtypeStruct((pairs, rows // BLK, 8, 2 * BLK), jnp.float32)
    return pl.pallas_call(
        near_kernel,
        out_shape=(jax.ShapeDtypeStruct((width, rows), jnp.float32), stat, stat),
        grid=(pairs,),
        in_specs=[tall, k_spec, vt_spec, pl.BlockSpec(mask.shape, lambda i: (0, 0, 0))],
        out_specs=(tall, row, row),
        name="near_attention",
    )(qt, k, vt, mask)


def far_attention(qt, k, vt, parts):
    width, rows = qt.shape
    tall, k_spec, vt_spec, row = pair_specs(rows, k.shape[0])
    return pl.pallas_call(
        far_kernel,
        out_shape=jax.ShapeDtypeStruct((width, rows), jnp.bfloat16),
        grid=(width // BLK,),
        in_specs=[tall, k_spec, vt_spec, tall, row, row],
        out_specs=tall,
        name="far_attention",
    )(qt, k, vt, *parts)


def run_copies(copies):
    for copy in copies:
        copy.start()
    for copy in copies:
        copy.wait()


def piece_kernel(core_ref, wt_ref, out_w_ref, piece_ref, sems):
    rows, cols = wt_ref.shape[0], piece_ref.shape[1]
    mine = pl.ds(pl.multiple_of(core_ref[0] * cols, cols), cols)
    run_copies(
        [
            pltpu.make_async_copy(wt_ref.at[:, mine], piece_ref.at[:rows], sems.at[0]),
            pltpu.make_async_copy(out_w_ref.at[:, mine], piece_ref.at[rows:], sems.at[1]),
        ]
    )


def any_specs(count):
    return [pl.BlockSpec(memory_space=pl.ANY)] * count


def own_piece(core, wt, out_w):
    rows = wt.shape[0] + out_w.shape[0]
    return pl.pallas_call(
        piece_kernel,
        out_shape=jax.ShapeDtypeStruct((rows, wt.shape[1] // 2), jnp.bfloat16),
        in_specs=[pl.BlockSpec(memory_space=pltpu.SMEM)] + any_specs(2),
        out_specs=pl.BlockSpec(memory_space=pltpu.VMEM),
        scratch_shapes=[pltpu.SemaphoreType.DMA((2,))],
        name="own_piece",
    )(core, wt, out_w)


def join_kernel(*refs):
    parts, out_ref, sems = refs[:-2], refs[-2], refs[-1]
    copies, row = [], 0
    for n, part in enumerate(parts):
        into = out_ref.at[pl.ds(row, part.shape[0])]
        copies.append(pltpu.make_async_copy(part, into, sems.at[n]))
        row += part.shape[0]
    run_copies(copies)


def join(*parts):
    rows = sum(part.shape[0] for part in parts)
    return pl.pallas_call(
        join_kernel,
        out_shape=jax.ShapeDtypeStruct((rows,) + parts[0].shape[1:], jnp.bfloat16),
        in_specs=any_specs(len(parts)),
        out_specs=pl.BlockSpec(memory_space=pltpu.VMEM),
        scratch_shapes=[pltpu.SemaphoreType.DMA((len(parts),))],
        name="join",
    )(*parts)


def assemble_kernel(core_ref, *refs):
    sems = refs[-1]
    outs, parts = refs[-5:-1], refs[:-5]
    hd, width = outs[0].shape[1], outs[0].shape[2]
    cols = width // 2
    half = len(parts) // 2
    copies = []
    for n, part in enumerate(parts):
        side = core_ref[0] if n < half else 1 - core_ref[0]
        into_cols = pl.ds(pl.multiple_of(side * cols, cols), cols)
        count = part.shape[0]
        into_heads = pl.ds((n % half) * count, count)
        for k, out in enumerate(outs):
            copies.append(
                pltpu.make_async_copy(
                    part.at[:, pl.ds(k * hd, hd)],
                    out.at[into_heads, :, into_cols],
                    sems.at[n * len(outs) + k],
                )
            )
    run_copies(copies)


def assemble(core, parts, heads):
    count, rows, cols = parts[0].shape
    hd = rows // 4
    one = jax.ShapeDtypeStruct((heads, hd, 2 * cols), jnp.bfloat16)
    return pl.pallas_call(
        assemble_kernel,
        out_shape=(one,) * 4,
        in_specs=[pl.BlockSpec(memory_space=pltpu.SMEM)] + any_specs(len(parts)),
        out_specs=(pl.BlockSpec(memory_space=pltpu.VMEM),) * 4,
        scratch_shapes=[pltpu.SemaphoreType.DMA((4 * len(parts),))],
        name="assemble",
    )(core, *parts)


def tied(value, *others):
    return lax.optimization_barrier((value,) + others)[0]


def shift(value, by, heads):
    pairs = [(i, (i + by) % heads) for i in range(heads)]
    return lax.ppermute(value, "head", pairs)


def swap(value, bits, devices):
    return lax.ppermute(value, ("ctx", "head"), [(i, i ^ bits) for i in range(devices)])


def exchange_plan(pairs_dev, pairs_off, ctx_count, ctx_index, lower, per_dev):
    pair_count = lower.shape[0]
    all_dev = pairs_dev.reshape(ctx_count, pair_count)
    all_off = pairs_off.reshape(ctx_count, pair_count)
    own = all_dev == ctx_index
    rank = jnp.sum((own[:, None, :] & lower[None]).astype(jnp.int32), axis=2)
    slot = jnp.arange(CAP, dtype=jnp.int32)
    chosen = own[:, None, :] & (rank[:, None, :] == slot[None, :, None])
    send = jnp.sum(jnp.where(chosen, all_off[:, None, :], 0), axis=2)
    send = jnp.pad(send, ((0, 0), (0, 1))).reshape(-1)
    own_dev = lax.dynamic_index_in_dim(all_dev, ctx_index, 0, keepdims=False)
    earlier = (own_dev[:, None] == own_dev[None, :]) & lower
    take = own_dev * SLOTS + jnp.sum(earlier.astype(jnp.int32), axis=1)
    take = jnp.pad(take.reshape(-1, per_dev), ((0, 0), (0, 1)), constant_values=CAP)
    return send, take.reshape(-1)


def window_mask(lengths, first_pos, doc_tokens, rows):
    line_end = jnp.cumsum(lengths)
    positions = first_pos - BLK + jnp.arange(rows + 2 * BLK, dtype=jnp.int32)
    line = jnp.sum((line_end[None, :] <= positions[:, None]).astype(jnp.int32), axis=1)
    inside = (positions >= 0) & (positions < doc_tokens)
    line = jnp.where(inside, line, -1)
    masks = []
    for b in range(rows // BLK):
        keys = line[b * BLK : (b + 3) * BLK]
        queries = line[(b + 1) * BLK : (b + 2) * BLK]
        masks.append(jnp.where(keys[:, None] == queries[None, :], 0.0, NEG))
    return jnp.stack(masks).astype(jnp.float32)


def per_device(
    tokens, ln_gain, ln_bias, qkv_weight, out_weight, out_bias, lengths, pairs_dev, pairs_off
):
    ctx_count = lax.axis_size("ctx")
    heads = lax.axis_size("head")
    devices = ctx_count * heads
    ctx_index = lax.axis_index("ctx")
    head_index = lax.axis_index("head")
    rows, width = tokens.shape
    hd = width // heads

    wt = jnp.transpose(qkv_weight[:, 0, :])
    core = (ctx_index % 2).astype(jnp.int32).reshape(1)
    place = ctx_index * heads + head_index

    normed_t = layer_norm(tokens, ln_gain, ln_bias, heads)
    cells = lax.all_to_all(normed_t, "head", split_axis=0, concat_axis=0, tiled=True)

    own = own_piece(core, wt, out_weight)
    u1, d1 = shift(own, 2, heads), shift(own, -2, heads)

    both = ("ctx", "head")
    right = [(i, i + 1) for i in range(devices - 1)]
    left = [(i + 1, i) for i in range(devices - 1)]
    before = lax.ppermute(normed_t[:, :, rows - BLK :], both, right)
    after = lax.ppermute(normed_t[:, :, :BLK], both, left)

    pair_count = (heads * rows // BLK) * RAND
    order = jnp.arange(pair_count, dtype=jnp.int32)
    lower = order[None, :] < order[:, None]
    send, take = exchange_plan(
        pairs_dev, pairs_off, ctx_count, ctx_index, lower, pair_count // heads
    )
    outgoing = pick_blocks(tied(send, u1, d1), cells)
    outgoing = outgoing.reshape(ctx_count, SLOTS * hd, BLK)
    slots = lax.all_to_all(outgoing, "ctx", split_axis=0, concat_axis=0, tiled=True)
    slots = slots.reshape(ctx_count * SLOTS, hd, BLK)

    mid = own.shape[0] // 2
    u2, d2 = shift(u1, 2, heads), shift(d1, -2, heads)
    u3, d3 = shift(u2, 2, heads), shift(d2, -2, heads)
    u4, d4 = shift(u3[:mid], 2, heads), shift(d3[mid:], -2, heads)
    shape = (heads // 4,) + own.shape
    a = join(own, u1, d1, u2).reshape(shape)
    b = join(d2, u3, d3, u4, d4).reshape(shape)
    c = swap(a, 1, devices)
    d = swap(b, 2 * heads + 1, devices)

    mine = [a, b, c, d]
    other = [swap(part, heads, devices) for part in mine]
    placed = place_blocks(tied(take, before, after, *other), slots, heads)
    far = lax.all_to_all(placed, "head", split_axis=0, concat_axis=0, tiled=True)
    far = far.reshape(width, far.shape[2])

    near = jnp.concatenate([before, normed_t, after], axis=2)
    near = near.reshape(width, near.shape[2])

    mask = window_mask(lengths, place * rows, devices * rows, rows)

    f32 = jnp.float32
    bf16 = jnp.bfloat16
    weights = assemble(core, mine + other, heads)
    w_q, w_k, w_v, w_o = (w.reshape(width, width) for w in weights)
    own_t = normed_t.reshape(width, rows)
    qt = jnp.dot(w_q, own_t, preferred_element_type=f32).astype(bf16)
    qt = (qt.astype(f32) * hd**-0.5).astype(bf16)
    k_near = lax.dot_general(near, w_k, TN, preferred_element_type=f32).astype(bf16)
    vt_near = jnp.dot(w_v, near, preferred_element_type=f32).astype(bf16)
    parts = near_attention(qt, k_near, vt_near, mask)
    k_far = lax.dot_general(far, w_k, TN, preferred_element_type=f32).astype(bf16)
    vt_far = jnp.dot(w_v, far, preferred_element_type=f32).astype(bf16)
    attended = far_attention(qt, k_far, vt_far, parts)
    projected = lax.dot_general(
        attended, w_o, (((0,), (0,)), ((), ())), preferred_element_type=f32
    )
    return (projected + out_bias).astype(bf16)


def solution(mesh):
    in_specs = (
        P(("ctx", "head"), None),
        P(),
        P(),
        P(None, "head", None),
        P("head", None),
        P(),
        P(),
        P(),
        P(),
    )
    return jax.shard_map(
        per_device,
        mesh=mesh,
        in_specs=in_specs,
        out_specs=P(("ctx", "head"), None),
        check_vma=False,
    )
```

```python
import jax
import jax.numpy as jnp
from jax import lax
from jax.experimental import pallas as pl
from jax.experimental.pallas import tpu as pltpu
from jax.sharding import PartitionSpec as P

BLK = 128
RAND = 3
CAP = 4
SLOTS = CAP + 1
EPS = 1e-05
NEG = float("-inf")
TN = (((0,), (1,)), ((), ()))


def ln_kernel(tok_ref, gain_ref, bias_ref, normt_ref, first_ref, last_ref):
    values = tok_ref[...].astype(jnp.float32)
    center = values - jnp.mean(values, axis=-1, keepdims=True)
    spread = jnp.mean(center * center, axis=-1, keepdims=True)
    normed = center * lax.rsqrt(spread + EPS) * gain_ref[...] + bias_ref[...]
    turned = jnp.transpose(normed).astype(jnp.bfloat16).reshape(normt_ref.shape)
    normt_ref[...] = turned
    first_ref[...] = turned[:, :, :BLK]
    last_ref[...] = turned[:, :, turned.shape[2] - BLK :]


def layer_norm(tokens, gain, bias, heads):
    rows, width = tokens.shape
    return pl.pallas_call(
        ln_kernel,
        out_shape=tuple(
            jax.ShapeDtypeStruct((heads, width // heads, cols), jnp.bfloat16)
            for cols in (rows, BLK, BLK)
        ),
        name="layer_norm",
    )(tokens, gain.reshape(1, width), bias.reshape(1, width))


def pick_kernel(ids_ref, cells_ref, out_ref):
    def step(slot, carry):
        block = ids_ref[slot]
        cols = pl.ds(pl.multiple_of((block % 2) * BLK, BLK), BLK)
        out_ref[slot] = cells_ref[block // 2, :, cols]
        return carry

    lax.fori_loop(0, out_ref.shape[0], step, 0, unroll=4)


def pick_blocks(ids, cells):
    return pl.pallas_call(
        pick_kernel,
        out_shape=jax.ShapeDtypeStruct((ids.shape[0], cells.shape[1], BLK), jnp.bfloat16),
        in_specs=[
            pl.BlockSpec(memory_space=pltpu.SMEM),
            pl.BlockSpec(memory_space=pltpu.VMEM),
        ],
        out_specs=pl.BlockSpec(memory_space=pltpu.VMEM),
        name="pick_blocks",
    )(ids, cells)


def place_kernel(pos_ref, slots_ref, out_ref):
    per_dev = out_ref.shape[2] // BLK

    def step(dev, carry):
        for j in range(per_dev):
            out_ref[dev, :, j * BLK : (j + 1) * BLK] = slots_ref[pos_ref[dev * per_dev + j]]
        return carry

    lax.fori_loop(0, out_ref.shape[0], step, 0)


def place_blocks(pos, slots, heads):
    per_dev = pos.shape[0] // heads
    return pl.pallas_call(
        place_kernel,
        out_shape=jax.ShapeDtypeStruct((heads, slots.shape[1], per_dev * BLK), jnp.bfloat16),
        in_specs=[
            pl.BlockSpec(memory_space=pltpu.SMEM),
            pl.BlockSpec(memory_space=pltpu.VMEM),
        ],
        out_specs=pl.BlockSpec(memory_space=pltpu.VMEM),
        name="place_blocks",
    )(pos, slots)


def both_heads(qt_pair):
    half = qt_pair.shape[0] // 2
    none = jnp.zeros((half, qt_pair.shape[1]), qt_pair.dtype)
    top = jnp.concatenate([qt_pair[:half], none], axis=1)
    return jnp.concatenate([top, jnp.concatenate([none, qt_pair[half:]], axis=1)], axis=0)


def own_halves(wide):
    half, cols = wide.shape[0] // 2, wide.shape[1] // 2
    return jnp.concatenate([wide[:half, :cols], wide[half:, cols:]], axis=0)


def spread_rows(row, half):
    cols = row.shape[1] // 2
    top = jnp.broadcast_to(row[:, :cols], (half, cols))
    return jnp.concatenate([top, jnp.broadcast_to(row[:, cols:], (half, cols))], axis=0)


def near_kernel(qt_ref, k_ref, vt_ref, mask_ref, acc_ref, top_ref, sum_ref):
    f32 = jnp.float32
    for b in range(2):
        cols = slice(b * BLK, (b + 1) * BLK)
        near = slice(b * BLK, (b + 3) * BLK)
        q = both_heads(qt_ref[:, cols])
        mask = mask_ref[b]
        s = jnp.dot(k_ref[near, :], q, preferred_element_type=f32)
        s = s + jnp.concatenate([mask, mask], axis=1)
        top = jnp.max(s, axis=0, keepdims=True)
        p = jnp.exp(s - top)
        total = jnp.sum(p, axis=0, keepdims=True)
        acc = jnp.dot(vt_ref[:, near], p.astype(jnp.bfloat16), preferred_element_type=f32)
        acc_ref[:, cols] = own_halves(acc)
        top_ref[0, b] = jnp.broadcast_to(top, top_ref.shape[2:])
        sum_ref[0, b] = jnp.broadcast_to(total, sum_ref.shape[2:])


def far_kernel(qt_ref, k_ref, vt_ref, acc_ref, top_ref, sum_ref, out_ref):
    f32 = jnp.float32
    spread = RAND * BLK
    shared = slice(2 * spread, 2 * spread + BLK)
    for b in range(2):
        cols = slice(b * BLK, (b + 1) * BLK)
        far = slice(b * spread, (b + 1) * spread)
        q = both_heads(qt_ref[:, cols])
        s = jnp.dot(k_ref[far, :], q, preferred_element_type=f32)
        g = jnp.dot(k_ref[shared, :], q, preferred_element_type=f32)
        old_top = top_ref[0, b, :1]
        top = jnp.maximum(jnp.max(s, axis=0, keepdims=True), old_top)
        top = jnp.maximum(jnp.max(g, axis=0, keepdims=True), top)
        p = jnp.exp(s - top)
        pg = jnp.exp(g - top)
        scale = jnp.exp(old_top - top)
        total = jnp.sum(p, axis=0, keepdims=True) + sum_ref[0, b, :1] * scale
        total += jnp.sum(pg, axis=0, keepdims=True)
        acc = jnp.dot(vt_ref[:, far], p.astype(jnp.bfloat16), preferred_element_type=f32)
        acc += jnp.dot(vt_ref[:, shared], pg.astype(jnp.bfloat16), preferred_element_type=f32)
        half = acc.shape[0] // 2
        acc = own_halves(acc) + acc_ref[:, cols] * spread_rows(scale, half)
        out_ref[:, cols] = (acc / spread_rows(total, half)).astype(jnp.bfloat16)


def pair_specs(rows, keys):
    tall = pl.BlockSpec((BLK, rows), lambda i: (i, 0))
    k_spec = pl.BlockSpec((keys, BLK), lambda i: (0, i))
    vt_spec = pl.BlockSpec((BLK, keys), lambda i: (i, 0))
    row = pl.BlockSpec((1, rows // BLK, 8, 2 * BLK), lambda i: (i, 0, 0, 0))
    return tall, k_spec, vt_spec, row


def near_attention(qt, k, vt, mask):
    width, rows = qt.shape
    pairs = width // BLK
    tall, k_spec, vt_spec, row = pair_specs(rows, k.shape[0])
    stat = jax.ShapeDtypeStruct((pairs, rows // BLK, 8, 2 * BLK), jnp.float32)
    return pl.pallas_call(
        near_kernel,
        out_shape=(jax.ShapeDtypeStruct((width, rows), jnp.float32), stat, stat),
        grid=(pairs,),
        in_specs=[tall, k_spec, vt_spec, pl.BlockSpec(mask.shape, lambda i: (0, 0, 0))],
        out_specs=(tall, row, row),
        name="near_attention",
    )(qt, k, vt, mask)


def far_attention(qt, k, vt, parts):
    width, rows = qt.shape
    tall, k_spec, vt_spec, row = pair_specs(rows, k.shape[0])
    return pl.pallas_call(
        far_kernel,
        out_shape=jax.ShapeDtypeStruct((width, rows), jnp.bfloat16),
        grid=(width // BLK,),
        in_specs=[tall, k_spec, vt_spec, tall, row, row],
        out_specs=tall,
        name="far_attention",
    )(qt, k, vt, *parts)


def run_copies(copies):
    for copy in copies:
        copy.start()
    for copy in copies:
        copy.wait()


def piece_kernel(core_ref, wt_ref, out_w_ref, piece_ref, sems):
    rows, cols = wt_ref.shape[0], piece_ref.shape[1]
    mine = pl.ds(pl.multiple_of(core_ref[0] * cols, cols), cols)
    run_copies(
        [
            pltpu.make_async_copy(wt_ref.at[:, mine], piece_ref.at[:rows], sems.at[0]),
            pltpu.make_async_copy(out_w_ref.at[:, mine], piece_ref.at[rows:], sems.at[1]),
        ]
    )


def any_specs(count):
    return [pl.BlockSpec(memory_space=pl.ANY)] * count


def own_piece(core, wt, out_w):
    rows = wt.shape[0] + out_w.shape[0]
    return pl.pallas_call(
        piece_kernel,
        out_shape=jax.ShapeDtypeStruct((rows, wt.shape[1] // 2), jnp.bfloat16),
        in_specs=[pl.BlockSpec(memory_space=pltpu.SMEM)] + any_specs(2),
        out_specs=pl.BlockSpec(memory_space=pltpu.VMEM),
        scratch_shapes=[pltpu.SemaphoreType.DMA((2,))],
        name="own_piece",
    )(core, wt, out_w)


def join_kernel(*refs):
    parts, out_ref, sems = refs[:-2], refs[-2], refs[-1]
    copies, row = [], 0
    for n, part in enumerate(parts):
        into = out_ref.at[pl.ds(row, part.shape[0])]
        copies.append(pltpu.make_async_copy(part, into, sems.at[n]))
        row += part.shape[0]
    run_copies(copies)


def join(*parts):
    rows = sum(part.shape[0] for part in parts)
    return pl.pallas_call(
        join_kernel,
        out_shape=jax.ShapeDtypeStruct((rows,) + parts[0].shape[1:], jnp.bfloat16),
        in_specs=any_specs(len(parts)),
        out_specs=pl.BlockSpec(memory_space=pltpu.VMEM),
        scratch_shapes=[pltpu.SemaphoreType.DMA((len(parts),))],
        name="join",
    )(*parts)


def assemble_kernel(core_ref, *refs):
    sems = refs[-1]
    outs, parts = refs[-5:-1], refs[:-5]
    heads, hd, width = outs[0].shape
    cols = width // 2
    copies, head = [], 0
    for n, part in enumerate(parts):
        side = core_ref[0] if head < heads else 1 - core_ref[0]
        into_cols = pl.ds(pl.multiple_of(side * cols, cols), cols)
        count = part.shape[0]
        into_heads = pl.ds(head % heads, count)
        head += count
        for k, out in enumerate(outs):
            copies.append(
                pltpu.make_async_copy(
                    part.at[:, pl.ds(k * hd, hd)],
                    out.at[into_heads, :, into_cols],
                    sems.at[n * len(outs) + k],
                )
            )
    run_copies(copies)


def assemble(core, parts, heads, hd):
    cols = parts[0].shape[1]
    parts = [part.reshape(-1, 4 * hd, cols) for part in parts]
    one = jax.ShapeDtypeStruct((heads, hd, 2 * cols), jnp.bfloat16)
    return pl.pallas_call(
        assemble_kernel,
        out_shape=(one,) * 4,
        in_specs=[pl.BlockSpec(memory_space=pltpu.SMEM)] + any_specs(len(parts)),
        out_specs=(pl.BlockSpec(memory_space=pltpu.VMEM),) * 4,
        scratch_shapes=[pltpu.SemaphoreType.DMA((4 * len(parts),))],
        name="assemble",
    )(core, *parts)


def tied(value, *others):
    return lax.optimization_barrier((value,) + others)[0]


def shift(value, by, heads):
    pairs = [(i, (i + by) % heads) for i in range(heads)]
    return lax.ppermute(value, "head", pairs)


def swap(value, bits, devices):
    return lax.ppermute(value, ("ctx", "head"), [(i, i ^ bits) for i in range(devices)])


def exchange_plan(pairs_dev, pairs_off, ctx_count, ctx_index, lower, per_dev):
    pair_count = lower.shape[0]
    all_dev = pairs_dev.reshape(ctx_count, pair_count)
    all_off = pairs_off.reshape(ctx_count, pair_count)
    own = all_dev == ctx_index
    rank = jnp.sum((own[:, None, :] & lower[None]).astype(jnp.int32), axis=2)
    slot = jnp.arange(CAP, dtype=jnp.int32)
    chosen = own[:, None, :] & (rank[:, None, :] == slot[None, :, None])
    send = jnp.sum(jnp.where(chosen, all_off[:, None, :], 0), axis=2)
    send = jnp.pad(send, ((0, 0), (0, 1))).reshape(-1)
    own_dev = lax.dynamic_index_in_dim(all_dev, ctx_index, 0, keepdims=False)
    earlier = (own_dev[:, None] == own_dev[None, :]) & lower
    take = own_dev * SLOTS + jnp.sum(earlier.astype(jnp.int32), axis=1)
    take = jnp.pad(take.reshape(-1, per_dev), ((0, 0), (0, 1)), constant_values=CAP)
    return send, take.reshape(-1)


def window_mask(lengths, first_pos, doc_tokens, rows):
    line_end = jnp.cumsum(lengths)
    positions = first_pos - BLK + jnp.arange(rows + 2 * BLK, dtype=jnp.int32)
    line = jnp.sum((line_end[None, :] <= positions[:, None]).astype(jnp.int32), axis=1)
    inside = (positions >= 0) & (positions < doc_tokens)
    line = jnp.where(inside, line, -1)
    masks = []
    for b in range(rows // BLK):
        keys = line[b * BLK : (b + 3) * BLK]
        queries = line[(b + 1) * BLK : (b + 2) * BLK]
        masks.append(jnp.where(keys[:, None] == queries[None, :], 0.0, NEG))
    return jnp.stack(masks).astype(jnp.float32)


def per_device(
    tokens, ln_gain, ln_bias, qkv_weight, out_weight, out_bias, lengths, pairs_dev, pairs_off
):
    ctx_count = lax.axis_size("ctx")
    heads = lax.axis_size("head")
    devices = ctx_count * heads
    ctx_index = lax.axis_index("ctx")
    head_index = lax.axis_index("head")
    rows, width = tokens.shape
    hd = width // heads

    wt = jnp.transpose(qkv_weight[:, 0, :])
    core = (ctx_index % 2).astype(jnp.int32).reshape(1)
    place = ctx_index * heads + head_index

    normed_t, first, last = layer_norm(tokens, ln_gain, ln_bias, heads)
    cells = lax.all_to_all(normed_t, "head", split_axis=0, concat_axis=0, tiled=True)

    own = own_piece(core, wt, out_weight)
    beside = swap(own, 1, devices)

    both = ("ctx", "head")
    right = [(i, i + 1) for i in range(devices - 1)]
    left = [(i + 1, i) for i in range(devices - 1)]
    before = lax.ppermute(last, both, right)
    after = lax.ppermute(first, both, left)

    pair_count = (heads * rows // BLK) * RAND
    order = jnp.arange(pair_count, dtype=jnp.int32)
    lower = order[None, :] < order[:, None]
    send, take = exchange_plan(
        pairs_dev, pairs_off, ctx_count, ctx_index, lower, pair_count // heads
    )
    outgoing = pick_blocks(tied(send, beside, before, after), cells)
    outgoing = outgoing.reshape(ctx_count, SLOTS * hd, BLK)
    slots = lax.all_to_all(outgoing, "ctx", split_axis=0, concat_axis=0, tiled=True)
    slots = slots.reshape(ctx_count * SLOTS, hd, BLK)

    mid = own.shape[0]
    two = join(own, beside)
    u1, d1 = shift(two, 2, heads), shift(two, -2, heads)
    u2, d2 = shift(u1, 2, heads), shift(d1, -2, heads)
    u3, d3 = shift(u2, 2, heads), shift(d2, -2, heads)
    u4, d4 = shift(u3[:mid], 2, heads), shift(d3[mid:], -2, heads)
    mine = [two, u1, d1, u2, d2, u3, d3, u4, d4]
    other = [swap(join(*part), heads, devices) for part in (mine[:4], mine[4:])]
    placed = place_blocks(tied(take, *other), slots, heads)
    far = lax.all_to_all(placed, "head", split_axis=0, concat_axis=0, tiled=True)
    far = far.reshape(width, far.shape[2])

    near = jnp.concatenate([before, normed_t, after], axis=2)
    near = near.reshape(width, near.shape[2])

    mask = window_mask(lengths, place * rows, devices * rows, rows)

    f32 = jnp.float32
    bf16 = jnp.bfloat16
    weights = assemble(core, mine + other, heads, hd)
    w_q, w_k, w_v, w_o = (w.reshape(width, width) for w in weights)
    own_t = normed_t.reshape(width, rows)
    qt = jnp.dot(w_q, own_t, preferred_element_type=f32).astype(bf16)
    qt = (qt.astype(f32) * hd**-0.5).astype(bf16)
    k_near = lax.dot_general(near, w_k, TN, preferred_element_type=f32).astype(bf16)
    vt_near = jnp.dot(w_v, near, preferred_element_type=f32).astype(bf16)
    parts = near_attention(qt, k_near, vt_near, mask)
    k_far = lax.dot_general(far, w_k, TN, preferred_element_type=f32).astype(bf16)
    vt_far = jnp.dot(w_v, far, preferred_element_type=f32).astype(bf16)
    attended = far_attention(qt, k_far, vt_far, parts)
    projected = lax.dot_general(
        attended, w_o, (((0,), (0,)), ((), ())), preferred_element_type=f32
    )
    return (projected + out_bias).astype(bf16)


def solution(mesh):
    in_specs = (
        P(("ctx", "head"), None),
        P(),
        P(),
        P(None, "head", None),
        P("head", None),
        P(),
        P(),
        P(),
        P(),
    )
    return jax.shard_map(
        per_device,
        mesh=mesh,
        in_specs=in_specs,
        out_specs=P(("ctx", "head"), None),
        check_vma=False,
    )
```

```python
import jax
import jax.numpy as jnp
from jax import lax
from jax.experimental import pallas as pl
from jax.experimental.pallas import tpu as pltpu
from jax.sharding import PartitionSpec as P

BLK = 128
RAND = 3
CAP = 4
SLOTS = CAP + 1
EPS = 1e-05
NEG = float("-inf")
TN = (((0,), (1,)), ((), ()))


def ln_kernel(tok_ref, gain_ref, bias_ref, normt_ref, first_ref, last_ref):
    values = tok_ref[...].astype(jnp.float32)
    center = values - jnp.mean(values, axis=-1, keepdims=True)
    spread = jnp.mean(center * center, axis=-1, keepdims=True)
    normed = center * lax.rsqrt(spread + EPS) * gain_ref[...] + bias_ref[...]
    turned = jnp.transpose(normed).astype(jnp.bfloat16).reshape(normt_ref.shape)
    normt_ref[...] = turned
    first_ref[...] = turned[:, :, :BLK]
    last_ref[...] = turned[:, :, turned.shape[2] - BLK :]


def layer_norm(tokens, gain, bias, heads):
    rows, width = tokens.shape
    return pl.pallas_call(
        ln_kernel,
        out_shape=tuple(
            jax.ShapeDtypeStruct((heads, width // heads, cols), jnp.bfloat16)
            for cols in (rows, BLK, BLK)
        ),
        name="layer_norm",
    )(tokens, gain.reshape(1, width), bias.reshape(1, width))


def pick_kernel(ids_ref, cells_ref, out_ref):
    def step(slot, carry):
        block = ids_ref[slot]
        cols = pl.ds(pl.multiple_of((block % 2) * BLK, BLK), BLK)
        out_ref[slot] = cells_ref[block // 2, :, cols]
        return carry

    lax.fori_loop(0, out_ref.shape[0], step, 0, unroll=4)


def pick_blocks(ids, cells):
    return pl.pallas_call(
        pick_kernel,
        out_shape=jax.ShapeDtypeStruct((ids.shape[0], cells.shape[1], BLK), jnp.bfloat16),
        in_specs=[
            pl.BlockSpec(memory_space=pltpu.SMEM),
            pl.BlockSpec(memory_space=pltpu.VMEM),
        ],
        out_specs=pl.BlockSpec(memory_space=pltpu.VMEM),
        name="pick_blocks",
    )(ids, cells)


def place_kernel(pos_ref, slots_ref, out_ref):
    per_dev = out_ref.shape[2] // BLK

    def step(dev, carry):
        for j in range(per_dev):
            out_ref[dev, :, j * BLK : (j + 1) * BLK] = slots_ref[pos_ref[dev * per_dev + j]]
        return carry

    lax.fori_loop(0, out_ref.shape[0], step, 0)


def place_blocks(pos, slots, heads):
    per_dev = pos.shape[0] // heads
    return pl.pallas_call(
        place_kernel,
        out_shape=jax.ShapeDtypeStruct((heads, slots.shape[1], per_dev * BLK), jnp.bfloat16),
        in_specs=[
            pl.BlockSpec(memory_space=pltpu.SMEM),
            pl.BlockSpec(memory_space=pltpu.VMEM),
        ],
        out_specs=pl.BlockSpec(memory_space=pltpu.VMEM),
        name="place_blocks",
    )(pos, slots)


def both_heads(qt_pair):
    half = qt_pair.shape[0] // 2
    none = jnp.zeros((half, qt_pair.shape[1]), qt_pair.dtype)
    top = jnp.concatenate([qt_pair[:half], none], axis=1)
    return jnp.concatenate([top, jnp.concatenate([none, qt_pair[half:]], axis=1)], axis=0)


def own_halves(wide):
    half, cols = wide.shape[0] // 2, wide.shape[1] // 2
    return jnp.concatenate([wide[:half, :cols], wide[half:, cols:]], axis=0)


def spread_rows(row, half):
    cols = row.shape[1] // 2
    top = jnp.broadcast_to(row[:, :cols], (half, cols))
    return jnp.concatenate([top, jnp.broadcast_to(row[:, cols:], (half, cols))], axis=0)


def near_kernel(qt_ref, k_ref, vt_ref, mask_ref, acc_ref, top_ref, sum_ref):
    f32 = jnp.float32
    for b in range(2):
        cols = slice(b * BLK, (b + 1) * BLK)
        near = slice(b * BLK, (b + 3) * BLK)
        q = both_heads(qt_ref[:, cols])
        mask = mask_ref[b]
        s = jnp.dot(k_ref[near, :], q, preferred_element_type=f32)
        s = s + jnp.concatenate([mask, mask], axis=1)
        top = jnp.max(s, axis=0, keepdims=True)
        p = jnp.exp(s - top)
        total = jnp.sum(p, axis=0, keepdims=True)
        acc = jnp.dot(vt_ref[:, near], p.astype(jnp.bfloat16), preferred_element_type=f32)
        acc_ref[:, cols] = own_halves(acc)
        top_ref[0, b] = jnp.broadcast_to(top, top_ref.shape[2:])
        sum_ref[0, b] = jnp.broadcast_to(total, sum_ref.shape[2:])


def far_kernel(qt_ref, k_ref, vt_ref, acc_ref, top_ref, sum_ref, out_ref):
    f32 = jnp.float32
    spread = RAND * BLK
    shared = slice(2 * spread, 2 * spread + BLK)
    for b in range(2):
        cols = slice(b * BLK, (b + 1) * BLK)
        far = slice(b * spread, (b + 1) * spread)
        q = both_heads(qt_ref[:, cols])
        s = jnp.dot(k_ref[far, :], q, preferred_element_type=f32)
        g = jnp.dot(k_ref[shared, :], q, preferred_element_type=f32)
        old_top = top_ref[0, b, :1]
        top = jnp.maximum(jnp.max(s, axis=0, keepdims=True), old_top)
        top = jnp.maximum(jnp.max(g, axis=0, keepdims=True), top)
        p = jnp.exp(s - top)
        pg = jnp.exp(g - top)
        scale = jnp.exp(old_top - top)
        total = jnp.sum(p, axis=0, keepdims=True) + sum_ref[0, b, :1] * scale
        total += jnp.sum(pg, axis=0, keepdims=True)
        acc = jnp.dot(vt_ref[:, far], p.astype(jnp.bfloat16), preferred_element_type=f32)
        acc += jnp.dot(vt_ref[:, shared], pg.astype(jnp.bfloat16), preferred_element_type=f32)
        half = acc.shape[0] // 2
        acc = own_halves(acc) + acc_ref[:, cols] * spread_rows(scale, half)
        out_ref[:, cols] = (acc / spread_rows(total, half)).astype(jnp.bfloat16)


def pair_specs(rows, keys):
    tall = pl.BlockSpec((BLK, rows), lambda i: (i, 0))
    k_spec = pl.BlockSpec((keys, BLK), lambda i: (0, i))
    vt_spec = pl.BlockSpec((BLK, keys), lambda i: (i, 0))
    row = pl.BlockSpec((1, rows // BLK, 8, 2 * BLK), lambda i: (i, 0, 0, 0))
    return tall, k_spec, vt_spec, row


def near_attention(qt, k, vt, mask):
    width, rows = qt.shape
    pairs = width // BLK
    tall, k_spec, vt_spec, row = pair_specs(rows, k.shape[0])
    stat = jax.ShapeDtypeStruct((pairs, rows // BLK, 8, 2 * BLK), jnp.float32)
    return pl.pallas_call(
        near_kernel,
        out_shape=(jax.ShapeDtypeStruct((width, rows), jnp.float32), stat, stat),
        grid=(pairs,),
        in_specs=[tall, k_spec, vt_spec, pl.BlockSpec(mask.shape, lambda i: (0, 0, 0))],
        out_specs=(tall, row, row),
        name="near_attention",
    )(qt, k, vt, mask)


def far_attention(qt, k, vt, parts):
    width, rows = qt.shape
    tall, k_spec, vt_spec, row = pair_specs(rows, k.shape[0])
    return pl.pallas_call(
        far_kernel,
        out_shape=jax.ShapeDtypeStruct((width, rows), jnp.bfloat16),
        grid=(width // BLK,),
        in_specs=[tall, k_spec, vt_spec, tall, row, row],
        out_specs=tall,
        name="far_attention",
    )(qt, k, vt, *parts)


def run_copies(copies):
    for copy in copies:
        copy.start()
    for copy in copies:
        copy.wait()


def piece_kernel(core_ref, wt_ref, out_w_ref, piece_ref, sems):
    rows, cols = wt_ref.shape[0], piece_ref.shape[1]
    mine = pl.ds(pl.multiple_of(core_ref[0] * cols, cols), cols)
    run_copies(
        [
            pltpu.make_async_copy(wt_ref.at[:, mine], piece_ref.at[:rows], sems.at[0]),
            pltpu.make_async_copy(out_w_ref.at[:, mine], piece_ref.at[rows:], sems.at[1]),
        ]
    )


def any_specs(count):
    return [pl.BlockSpec(memory_space=pl.ANY)] * count


def own_piece(core, wt, out_w):
    rows = wt.shape[0] + out_w.shape[0]
    return pl.pallas_call(
        piece_kernel,
        out_shape=jax.ShapeDtypeStruct((rows, wt.shape[1] // 2), jnp.bfloat16),
        in_specs=[pl.BlockSpec(memory_space=pltpu.SMEM)] + any_specs(2),
        out_specs=pl.BlockSpec(memory_space=pltpu.VMEM),
        scratch_shapes=[pltpu.SemaphoreType.DMA((2,))],
        name="own_piece",
    )(core, wt, out_w)


def assemble_kernel(core_ref, *refs):
    sems = refs[-1]
    outs, parts = refs[-5:-1], refs[:-5]
    heads, hd, width = outs[0].shape
    cols = width // 2
    copies, head = [], 0
    for n, part in enumerate(parts):
        side = core_ref[0] if head < heads else 1 - core_ref[0]
        into_cols = pl.ds(pl.multiple_of(side * cols, cols), cols)
        count = part.shape[0]
        into_heads = pl.ds(head % heads, count)
        head += count
        for k, out in enumerate(outs):
            copies.append(
                pltpu.make_async_copy(
                    part.at[:, pl.ds(k * hd, hd)],
                    out.at[into_heads, :, into_cols],
                    sems.at[n * len(outs) + k],
                )
            )
    run_copies(copies)


def assemble(core, parts, heads, hd):
    cols = parts[0].shape[2]
    one = jax.ShapeDtypeStruct((heads, hd, 2 * cols), jnp.bfloat16)
    return pl.pallas_call(
        assemble_kernel,
        out_shape=(one,) * 4,
        in_specs=[pl.BlockSpec(memory_space=pltpu.SMEM)] + any_specs(len(parts)),
        out_specs=(pl.BlockSpec(memory_space=pltpu.VMEM),) * 4,
        scratch_shapes=[pltpu.SemaphoreType.DMA((4 * len(parts),))],
        name="assemble",
    )(core, *parts)


def tied(value, *others):
    return lax.optimization_barrier((value,) + others)[0]


def swap(value, bits, devices):
    return lax.ppermute(value, ("ctx", "head"), [(i, i ^ bits) for i in range(devices)])


def exchange_plan(pairs_dev, pairs_off, ctx_count, ctx_index, lower, per_dev):
    pair_count = lower.shape[0]
    all_dev = pairs_dev.reshape(ctx_count, pair_count)
    all_off = pairs_off.reshape(ctx_count, pair_count)
    own = all_dev == ctx_index
    rank = jnp.sum((own[:, None, :] & lower[None]).astype(jnp.int32), axis=2)
    slot = jnp.arange(CAP, dtype=jnp.int32)
    chosen = own[:, None, :] & (rank[:, None, :] == slot[None, :, None])
    send = jnp.sum(jnp.where(chosen, all_off[:, None, :], 0), axis=2)
    send = jnp.pad(send, ((0, 0), (0, 1))).reshape(-1)
    own_dev = lax.dynamic_index_in_dim(all_dev, ctx_index, 0, keepdims=False)
    earlier = (own_dev[:, None] == own_dev[None, :]) & lower
    take = own_dev * SLOTS + jnp.sum(earlier.astype(jnp.int32), axis=1)
    take = jnp.pad(take.reshape(-1, per_dev), ((0, 0), (0, 1)), constant_values=CAP)
    return send, take.reshape(-1)


def window_mask(lengths, first_pos, doc_tokens, rows):
    line_end = jnp.cumsum(lengths)
    positions = first_pos - BLK + jnp.arange(rows + 2 * BLK, dtype=jnp.int32)
    line = jnp.sum((line_end[None, :] <= positions[:, None]).astype(jnp.int32), axis=1)
    inside = (positions >= 0) & (positions < doc_tokens)
    line = jnp.where(inside, line, -1)
    masks = []
    for b in range(rows // BLK):
        keys = line[b * BLK : (b + 3) * BLK]
        queries = line[(b + 1) * BLK : (b + 2) * BLK]
        masks.append(jnp.where(keys[:, None] == queries[None, :], 0.0, NEG))
    return jnp.stack(masks).astype(jnp.float32)


def per_device(
    tokens, ln_gain, ln_bias, qkv_weight, out_weight, out_bias, lengths, pairs_dev, pairs_off
):
    ctx_count = lax.axis_size("ctx")
    heads = lax.axis_size("head")
    devices = ctx_count * heads
    ctx_index = lax.axis_index("ctx")
    head_index = lax.axis_index("head")
    rows, width = tokens.shape
    hd = width // heads

    wt = jnp.transpose(qkv_weight[:, 0, :])
    core = (ctx_index % 2).astype(jnp.int32).reshape(1)
    place = ctx_index * heads + head_index

    normed_t, first, last = layer_norm(tokens, ln_gain, ln_bias, heads)
    cells = lax.all_to_all(normed_t, "head", split_axis=0, concat_axis=0, tiled=True)

    own = own_piece(core, wt, out_weight)
    along_y = [list(range(first_x, heads, 2)) for first_x in range(2)]
    column = lax.all_gather(own, "head", axis_index_groups=along_y)

    both = ("ctx", "head")
    right = [(i, i + 1) for i in range(devices - 1)]
    left = [(i + 1, i) for i in range(devices - 1)]
    before = lax.ppermute(last, both, right)
    after = lax.ppermute(first, both, left)

    pair_count = (heads * rows // BLK) * RAND
    order = jnp.arange(pair_count, dtype=jnp.int32)
    lower = order[None, :] < order[:, None]
    send, take = exchange_plan(
        pairs_dev, pairs_off, ctx_count, ctx_index, lower, pair_count // heads
    )
    outgoing = pick_blocks(tied(send, before, after), cells)
    outgoing = outgoing.reshape(ctx_count, SLOTS * hd, BLK)
    slots = lax.all_to_all(outgoing, "ctx", split_axis=0, concat_axis=0, tiled=True)
    slots = slots.reshape(ctx_count * SLOTS, hd, BLK)

    half = column.shape[0] // 2
    mine = [
        column,
        swap(column[:half], 1, devices),
        swap(column[half:], 2 * heads + 1, devices),
    ]
    other = [swap(part, heads, devices) for part in mine]
    placed = place_blocks(tied(take, mine[1], mine[2], other[0]), slots, heads)
    far = lax.all_to_all(placed, "head", split_axis=0, concat_axis=0, tiled=True)
    far = far.reshape(width, far.shape[2])

    near = jnp.concatenate([before, normed_t, after], axis=2)
    near = near.reshape(width, near.shape[2])

    mask = window_mask(lengths, place * rows, devices * rows, rows)

    f32 = jnp.float32
    bf16 = jnp.bfloat16
    weights = assemble(core, mine + other, heads, hd)
    w_q, w_k, w_v, w_o = (w.reshape(width, width) for w in weights)
    own_t = normed_t.reshape(width, rows)
    qt = jnp.dot(w_q, own_t, preferred_element_type=f32).astype(bf16)
    qt = (qt.astype(f32) * hd**-0.5).astype(bf16)
    k_near = lax.dot_general(near, w_k, TN, preferred_element_type=f32).astype(bf16)
    vt_near = jnp.dot(w_v, near, preferred_element_type=f32).astype(bf16)
    parts = near_attention(qt, k_near, vt_near, mask)
    k_far = lax.dot_general(far, w_k, TN, preferred_element_type=f32).astype(bf16)
    vt_far = jnp.dot(w_v, far, preferred_element_type=f32).astype(bf16)
    attended = far_attention(qt, k_far, vt_far, parts)
    projected = lax.dot_general(
        attended, w_o, (((0,), (0,)), ((), ())), preferred_element_type=f32
    )
    return (projected + out_bias).astype(bf16)


def solution(mesh):
    in_specs = (
        P(("ctx", "head"), None),
        P(),
        P(),
        P(None, "head", None),
        P("head", None),
        P(),
        P(),
        P(),
        P(),
    )
    return jax.shard_map(
        per_device,
        mesh=mesh,
        in_specs=in_specs,
        out_specs=P(("ctx", "head"), None),
        check_vma=False,
    )
```

```python
import jax
import jax.numpy as jnp
from jax import lax
from jax.experimental import pallas as pl
from jax.experimental.pallas import tpu as pltpu
from jax.sharding import PartitionSpec as P


BLK = 128
RAND = 3
CAP = 4
EPS = 1e-05
NEG = float("-inf")
TN = (((0,), (1,)), ((), ()))


def ln_kernel(tok_ref, gain_ref, bias_ref, normt_ref, first_ref, last_ref):
    values = tok_ref[...].astype(jnp.float32)
    center = values - jnp.mean(values, axis=-1, keepdims=True)
    spread = jnp.mean(center * center, axis=-1, keepdims=True)
    normed = center * lax.rsqrt(spread + EPS) * gain_ref[...] + bias_ref[...]
    turned = jnp.transpose(normed).astype(jnp.bfloat16).reshape(normt_ref.shape)
    normt_ref[...] = turned
    first_ref[...] = turned[:, :, :BLK]
    last_ref[...] = turned[:, :, turned.shape[2] - BLK :]


def layer_norm(tokens, gain, bias, heads):
    rows, width = tokens.shape
    return pl.pallas_call(
        ln_kernel,
        out_shape=tuple(
            jax.ShapeDtypeStruct((heads, width // heads, cols), jnp.bfloat16)
            for cols in (rows, BLK, BLK)
        ),
        name="layer_norm",
    )(tokens, gain.reshape(1, width), bias.reshape(1, width))


def pick_kernel(ids_ref, cells_ref, out_ref):
    def step(slot, carry):
        block = ids_ref[slot]
        cols = pl.ds(pl.multiple_of((block % 2) * BLK, BLK), BLK)
        out_ref[slot] = cells_ref[block // 2, :, cols]
        return carry

    lax.fori_loop(0, out_ref.shape[0], step, 0, unroll=4)


def pick_blocks(ids, cells):
    return pl.pallas_call(
        pick_kernel,
        out_shape=jax.ShapeDtypeStruct((ids.shape[0], cells.shape[1], BLK), jnp.bfloat16),
        in_specs=[
            pl.BlockSpec(memory_space=pltpu.SMEM),
            pl.BlockSpec(memory_space=pltpu.VMEM),
        ],
        out_specs=pl.BlockSpec(memory_space=pltpu.VMEM),
        name="pick_blocks",
    )(ids, cells)


def place_kernel(pos_ref, slots_ref, out_ref):
    per_dev = out_ref.shape[2] // BLK

    def step(dev, carry):
        for j in range(per_dev):
            out_ref[dev, :, j * BLK : (j + 1) * BLK] = slots_ref[pos_ref[dev * per_dev + j]]
        return carry

    lax.fori_loop(0, out_ref.shape[0], step, 0)


def place_blocks(pos, slots, heads):
    per_dev = pos.shape[0] // heads
    return pl.pallas_call(
        place_kernel,
        out_shape=jax.ShapeDtypeStruct((heads, slots.shape[1], per_dev * BLK), jnp.bfloat16),
        in_specs=[
            pl.BlockSpec(memory_space=pltpu.SMEM),
            pl.BlockSpec(memory_space=pltpu.VMEM),
        ],
        out_specs=pl.BlockSpec(memory_space=pltpu.VMEM),
        name="place_blocks",
    )(pos, slots)


def both_heads(qt_pair):
    half = qt_pair.shape[0] // 2
    none = jnp.zeros((half, qt_pair.shape[1]), qt_pair.dtype)
    top = jnp.concatenate([qt_pair[:half], none], axis=1)
    return jnp.concatenate([top, jnp.concatenate([none, qt_pair[half:]], axis=1)], axis=0)


def own_halves(wide):
    half, cols = wide.shape[0] // 2, wide.shape[1] // 2
    return jnp.concatenate([wide[:half, :cols], wide[half:, cols:]], axis=0)


def spread_rows(row, half):
    cols = row.shape[1] // 2
    top = jnp.broadcast_to(row[:, :cols], (half, cols))
    return jnp.concatenate([top, jnp.broadcast_to(row[:, cols:], (half, cols))], axis=0)


def near_kernel(qt_ref, k_ref, vt_ref, mask_ref, acc_ref, top_ref, sum_ref):
    f32 = jnp.float32
    shared = slice(4 * BLK, 5 * BLK)
    scores = []
    for b in range(2):
        near = slice(b * BLK, (b + 3) * BLK)
        q = both_heads(qt_ref[:, b * BLK : (b + 1) * BLK])
        mask = mask_ref[b]
        s = jnp.dot(k_ref[near, :], q, preferred_element_type=f32)
        s = s + jnp.concatenate([mask, mask], axis=1)
        scores.append((s, jnp.dot(k_ref[shared, :], q, preferred_element_type=f32)))
    for b, (s, g) in enumerate(scores):
        near = slice(b * BLK, (b + 3) * BLK)
        top = jnp.maximum(jnp.max(s, axis=0, keepdims=True), jnp.max(g, axis=0, keepdims=True))
        p = jnp.exp(s - top)
        pg = jnp.exp(g - top)
        total = jnp.sum(p, axis=0, keepdims=True) + jnp.sum(pg, axis=0, keepdims=True)
        acc = jnp.dot(vt_ref[:, near], p.astype(jnp.bfloat16), preferred_element_type=f32)
        acc += jnp.dot(vt_ref[:, shared], pg.astype(jnp.bfloat16), preferred_element_type=f32)
        acc_ref[:, b * BLK : (b + 1) * BLK] = own_halves(acc)
        top_ref[0, b] = jnp.broadcast_to(top, top_ref.shape[2:])
        sum_ref[0, b] = jnp.broadcast_to(total, sum_ref.shape[2:])


def far_kernel(qt_ref, k_ref, vt_ref, acc_ref, top_ref, sum_ref, out_ref):
    f32 = jnp.float32
    spread = RAND * BLK
    scores = []
    for b in range(2):
        q = both_heads(qt_ref[:, b * BLK : (b + 1) * BLK])
        keys = k_ref[b * spread : (b + 1) * spread, :]
        scores.append(jnp.dot(keys, q, preferred_element_type=f32))
    for b, s in enumerate(scores):
        cols = slice(b * BLK, (b + 1) * BLK)
        far = slice(b * spread, (b + 1) * spread)
        old_top = top_ref[0, b, :1]
        top = jnp.maximum(jnp.max(s, axis=0, keepdims=True), old_top)
        p = jnp.exp(s - top)
        scale = jnp.exp(old_top - top)
        total = jnp.sum(p, axis=0, keepdims=True) + sum_ref[0, b, :1] * scale
        acc = jnp.dot(vt_ref[:, far], p.astype(jnp.bfloat16), preferred_element_type=f32)
        half = acc.shape[0] // 2
        acc = own_halves(acc) + acc_ref[:, cols] * spread_rows(scale, half)
        out_ref[:, cols] = (acc / spread_rows(total, half)).astype(jnp.bfloat16)


def pair_specs(rows, keys):
    tall = pl.BlockSpec((BLK, rows), lambda i: (i, 0))
    k_spec = pl.BlockSpec((keys, BLK), lambda i: (0, i))
    vt_spec = pl.BlockSpec((BLK, keys), lambda i: (i, 0))
    row = pl.BlockSpec((1, rows // BLK, 8, 2 * BLK), lambda i: (i, 0, 0, 0))
    return tall, k_spec, vt_spec, row


def near_attention(qt, k, vt, mask):
    width, rows = qt.shape
    pairs = width // BLK
    tall, k_spec, vt_spec, row = pair_specs(rows, k.shape[0])
    stat = jax.ShapeDtypeStruct((pairs, rows // BLK, 8, 2 * BLK), jnp.float32)
    return pl.pallas_call(
        near_kernel,
        out_shape=(jax.ShapeDtypeStruct((width, rows), jnp.float32), stat, stat),
        grid=(pairs,),
        in_specs=[tall, k_spec, vt_spec, pl.BlockSpec(mask.shape, lambda i: (0, 0, 0))],
        out_specs=(tall, row, row),
        name="near_attention",
    )(qt, k, vt, mask)


def far_attention(qt, k, vt, parts):
    width, rows = qt.shape
    tall, k_spec, vt_spec, row = pair_specs(rows, k.shape[0])
    return pl.pallas_call(
        far_kernel,
        out_shape=jax.ShapeDtypeStruct((width, rows), jnp.bfloat16),
        grid=(width // BLK,),
        in_specs=[tall, k_spec, vt_spec, tall, row, row],
        out_specs=tall,
        name="far_attention",
    )(qt, k, vt, *parts)


def run_copies(copies):
    for copy in copies:
        copy.start()
    for copy in copies:
        copy.wait()


def piece_kernel(core_ref, wt_ref, out_w_ref, piece_ref, sems):
    rows, cols = wt_ref.shape[0], piece_ref.shape[1]
    mine = pl.ds(pl.multiple_of(core_ref[0] * cols, cols), cols)
    run_copies(
        [
            pltpu.make_async_copy(wt_ref.at[:, mine], piece_ref.at[:rows], sems.at[0]),
            pltpu.make_async_copy(out_w_ref.at[:, mine], piece_ref.at[rows:], sems.at[1]),
        ]
    )


def any_specs(count):
    return [pl.BlockSpec(memory_space=pl.ANY)] * count


def own_piece(core, wt, out_w):
    rows = wt.shape[0] + out_w.shape[0]
    return pl.pallas_call(
        piece_kernel,
        out_shape=jax.ShapeDtypeStruct((rows, wt.shape[1] // 2), jnp.bfloat16),
        in_specs=[pl.BlockSpec(memory_space=pltpu.SMEM)] + any_specs(2),
        out_specs=pl.BlockSpec(memory_space=pltpu.VMEM),
        scratch_shapes=[pltpu.SemaphoreType.DMA((2,))],
        name="own_piece",
    )(core, wt, out_w)


def assemble_kernel(core_ref, *refs):
    sems = refs[-1]
    outs, parts = refs[-5:-1], refs[:-5]
    heads, hd, width = outs[0].shape
    cols = width // 2
    copies, head = [], 0
    for n, part in enumerate(parts):
        side = core_ref[0] if head < heads else 1 - core_ref[0]
        into_cols = pl.ds(pl.multiple_of(side * cols, cols), cols)
        count = part.shape[0]
        into_heads = pl.ds(head % heads, count)
        head += count
        for k, out in enumerate(outs):
            copies.append(
                pltpu.make_async_copy(
                    part.at[:, pl.ds(k * hd, hd)],
                    out.at[into_heads, :, into_cols],
                    sems.at[n * len(outs) + k],
                )
            )
    run_copies(copies)


def assemble(core, parts, heads, hd):
    cols = parts[0].shape[2]
    one = jax.ShapeDtypeStruct((heads, hd, 2 * cols), jnp.bfloat16)
    return pl.pallas_call(
        assemble_kernel,
        out_shape=(one,) * 4,
        in_specs=[pl.BlockSpec(memory_space=pltpu.SMEM)] + any_specs(len(parts)),
        out_specs=(pl.BlockSpec(memory_space=pltpu.VMEM),) * 4,
        scratch_shapes=[pltpu.SemaphoreType.DMA((4 * len(parts),))],
        name="assemble",
    )(core, *parts)


def tied(value, *others):
    return lax.optimization_barrier((value,) + others)[0]


def swap(value, bits, devices):
    return lax.ppermute(value, ("ctx", "head"), [(i, i ^ bits) for i in range(devices)])


def exchange_plan(pairs_dev, pairs_off, ctx_count, ctx_index, lower):
    pair_count = lower.shape[0]
    all_dev = pairs_dev.reshape(ctx_count, pair_count)
    all_off = pairs_off.reshape(ctx_count, pair_count)
    own = all_dev == ctx_index
    rank = jnp.sum((own[:, None, :] & lower[None]).astype(jnp.int32), axis=2)
    slot = jnp.arange(CAP, dtype=jnp.int32)
    chosen = own[:, None, :] & (rank[:, None, :] == slot[None, :, None])
    send = jnp.sum(jnp.where(chosen, all_off[:, None, :], 0), axis=2)
    send = send.reshape(-1)
    own_dev = lax.dynamic_index_in_dim(all_dev, ctx_index, 0, keepdims=False)
    earlier = (own_dev[:, None] == own_dev[None, :]) & lower
    take = own_dev * CAP + jnp.sum(earlier.astype(jnp.int32), axis=1)
    return send, take


def window_mask(lengths, first_pos, doc_tokens, rows):
    line_end = jnp.cumsum(lengths)
    positions = first_pos - BLK + jnp.arange(rows + 2 * BLK, dtype=jnp.int32)
    line = jnp.sum((line_end[None, :] <= positions[:, None]).astype(jnp.int32), axis=1)
    inside = (positions >= 0) & (positions < doc_tokens)
    line = jnp.where(inside, line, -1)
    masks = []
    for b in range(rows // BLK):
        keys = line[b * BLK : (b + 3) * BLK]
        queries = line[(b + 1) * BLK : (b + 2) * BLK]
        masks.append(jnp.where(keys[:, None] == queries[None, :], 0.0, NEG))
    return jnp.stack(masks).astype(jnp.float32)


def per_device(
    tokens, ln_gain, ln_bias, qkv_weight, out_weight, out_bias, lengths, pairs_dev, pairs_off
):
    ctx_count = lax.axis_size("ctx")
    heads = lax.axis_size("head")
    devices = ctx_count * heads
    ctx_index = lax.axis_index("ctx")
    head_index = lax.axis_index("head")
    rows, width = tokens.shape
    hd = width // heads

    wt = jnp.transpose(qkv_weight[:, 0, :])
    core = (ctx_index % 2).astype(jnp.int32).reshape(1)
    place = ctx_index * heads + head_index

    normed_t, first, last = layer_norm(tokens, ln_gain, ln_bias, heads)
    cells = lax.all_to_all(normed_t, "head", split_axis=0, concat_axis=0, tiled=True)

    own = own_piece(core, wt, out_weight)
    along_y = [list(range(first_x, heads, 2)) for first_x in range(2)]
    column = lax.all_gather(own, "head", axis_index_groups=along_y)
    shared = jnp.where(place == 0, first, jnp.zeros_like(first))
    shared = lax.psum(tied(shared, own), ("ctx", "head"))

    both = ("ctx", "head")
    right = [(i, i + 1) for i in range(devices - 1)]
    left = [(i + 1, i) for i in range(devices - 1)]
    before = lax.ppermute(last, both, right)
    after = lax.ppermute(first, both, left)

    pair_count = (heads * rows // BLK) * RAND
    order = jnp.arange(pair_count, dtype=jnp.int32)
    lower = order[None, :] < order[:, None]
    send, take = exchange_plan(pairs_dev, pairs_off, ctx_count, ctx_index, lower)
    outgoing = pick_blocks(tied(send, before, after), cells)
    outgoing = outgoing.reshape(ctx_count, CAP * hd, BLK)
    slots = lax.all_to_all(outgoing, "ctx", split_axis=0, concat_axis=0, tiled=True)
    slots = slots.reshape(ctx_count * CAP, hd, BLK)

    half = column.shape[0] // 2
    mine = [
        column,
        swap(column[:half], 1, devices),
        swap(column[half:], 2 * heads + 1, devices),
    ]
    other = [swap(part, heads, devices) for part in mine]
    placed = place_blocks(tied(take, mine[1], mine[2], other[0]), slots, heads)
    far = lax.all_to_all(placed, "head", split_axis=0, concat_axis=0, tiled=True)
    far = far.reshape(width, far.shape[2])

    near = jnp.concatenate([before, normed_t, after, shared], axis=2)
    near = near.reshape(width, near.shape[2])

    mask = window_mask(lengths, place * rows, devices * rows, rows)

    f32 = jnp.float32
    bf16 = jnp.bfloat16
    weights = assemble(core, mine + other, heads, hd)
    w_q, w_k, w_v, w_o = (w.reshape(width, width) for w in weights)
    own_t = normed_t.reshape(width, rows)
    qt = jnp.dot(w_q, own_t, preferred_element_type=f32).astype(bf16)
    qt = (qt.astype(f32) * hd**-0.5).astype(bf16)
    k_near = lax.dot_general(near, w_k, TN, preferred_element_type=f32).astype(bf16)
    vt_near = jnp.dot(w_v, near, preferred_element_type=f32).astype(bf16)
    parts = near_attention(qt, k_near, vt_near, mask)
    k_far = lax.dot_general(far, w_k, TN, preferred_element_type=f32).astype(bf16)
    vt_far = jnp.dot(w_v, far, preferred_element_type=f32).astype(bf16)
    attended = far_attention(qt, k_far, vt_far, parts)
    projected = lax.dot_general(
        attended, w_o, (((0,), (0,)), ((), ())), preferred_element_type=f32
    )
    return (projected + out_bias).astype(bf16)


def solution(mesh):
    in_specs = (
        P(("ctx", "head"), None),
        P(),
        P(),
        P(None, "head", None),
        P("head", None),
        P(),
        P(),
        P(),
        P(),
    )
    return jax.shard_map(
        per_device,
        mesh=mesh,
        in_specs=in_specs,
        out_specs=P(("ctx", "head"), None),
        check_vma=False,
    )
```

```python
import jax
import jax.numpy as jnp
from jax import lax
from jax.experimental import pallas as pl
from jax.experimental.pallas import tpu as pltpu
from jax.sharding import PartitionSpec as P


BLK = 128
RAND = 3
CAP = 4
EPS = 1e-05
NEG = float("-inf")
TN = (((0,), (1,)), ((), ()))


def ln_kernel(tok_ref, gain_ref, bias_ref, normt_ref, first_ref, last_ref):
    values = tok_ref[...].astype(jnp.float32)
    center = values - jnp.mean(values, axis=-1, keepdims=True)
    spread = jnp.mean(center * center, axis=-1, keepdims=True)
    normed = center * lax.rsqrt(spread + EPS) * gain_ref[...] + bias_ref[...]
    turned = jnp.transpose(normed).astype(jnp.bfloat16).reshape(normt_ref.shape)
    normt_ref[...] = turned
    first_ref[...] = turned[:, :, :BLK]
    last_ref[...] = turned[:, :, turned.shape[2] - BLK :]


def layer_norm(tokens, gain, bias, heads):
    rows, width = tokens.shape
    return pl.pallas_call(
        ln_kernel,
        out_shape=tuple(
            jax.ShapeDtypeStruct((heads, width // heads, cols), jnp.bfloat16)
            for cols in (rows, BLK, BLK)
        ),
        name="layer_norm",
    )(tokens, gain.reshape(1, width), bias.reshape(1, width))


def pick_kernel(ids_ref, cells_ref, out_ref):
    def step(slot, carry):
        block = ids_ref[slot]
        cols = pl.ds(pl.multiple_of((block % 2) * BLK, BLK), BLK)
        out_ref[slot] = cells_ref[block // 2, :, cols]
        return carry

    lax.fori_loop(0, out_ref.shape[0], step, 0, unroll=4)


def pick_blocks(ids, cells):
    return pl.pallas_call(
        pick_kernel,
        out_shape=jax.ShapeDtypeStruct((ids.shape[0], cells.shape[1], BLK), jnp.bfloat16),
        in_specs=[
            pl.BlockSpec(memory_space=pltpu.SMEM),
            pl.BlockSpec(memory_space=pltpu.VMEM),
        ],
        out_specs=pl.BlockSpec(memory_space=pltpu.VMEM),
        name="pick_blocks",
    )(ids, cells)


def place_kernel(pos_ref, slots_ref, shared_ref, out_ref):
    per_dev = out_ref.shape[2] // BLK - 1

    def step(dev, carry):
        for j in range(per_dev):
            out_ref[dev, :, j * BLK : (j + 1) * BLK] = slots_ref[pos_ref[dev * per_dev + j]]
        out_ref[dev, :, per_dev * BLK :] = shared_ref[...]
        return carry

    lax.fori_loop(0, out_ref.shape[0], step, 0)


def place_blocks(pos, slots, shared, heads):
    cols = (pos.shape[0] // heads + 1) * BLK
    return pl.pallas_call(
        place_kernel,
        out_shape=jax.ShapeDtypeStruct((heads, slots.shape[1], cols), jnp.bfloat16),
        in_specs=[
            pl.BlockSpec(memory_space=pltpu.SMEM),
            pl.BlockSpec(memory_space=pltpu.VMEM),
            pl.BlockSpec(memory_space=pltpu.VMEM),
        ],
        out_specs=pl.BlockSpec(memory_space=pltpu.VMEM),
        name="place_blocks",
    )(pos, slots, shared)


def both_heads(qt_pair):
    half = qt_pair.shape[0] // 2
    none = jnp.zeros((half, qt_pair.shape[1]), qt_pair.dtype)
    top = jnp.concatenate([qt_pair[:half], none], axis=1)
    return jnp.concatenate([top, jnp.concatenate([none, qt_pair[half:]], axis=1)], axis=0)


def own_halves(wide):
    half, cols = wide.shape[0] // 2, wide.shape[1] // 2
    return jnp.concatenate([wide[:half, :cols], wide[half:, cols:]], axis=0)


def spread_rows(row, half):
    cols = row.shape[1] // 2
    top = jnp.broadcast_to(row[:, :cols], (half, cols))
    return jnp.concatenate([top, jnp.broadcast_to(row[:, cols:], (half, cols))], axis=0)


def near_kernel(qt_ref, k_ref, vt_ref, mask_ref, acc_ref, top_ref, sum_ref):
    f32 = jnp.float32
    scores = []
    for b in range(2):
        q = both_heads(qt_ref[:, b * BLK : (b + 1) * BLK])
        keys = k_ref[b * BLK : (b + 3) * BLK, :]
        mask = mask_ref[b]
        s = jnp.dot(keys, q, preferred_element_type=f32)
        scores.append(s + jnp.concatenate([mask, mask], axis=1))
    for b, s in enumerate(scores):
        top = jnp.max(s, axis=0, keepdims=True)
        p = jnp.exp(s - top)
        total = jnp.sum(p, axis=0, keepdims=True)
        near = slice(b * BLK, (b + 3) * BLK)
        acc = jnp.dot(vt_ref[:, near], p.astype(jnp.bfloat16), preferred_element_type=f32)
        acc_ref[:, b * BLK : (b + 1) * BLK] = own_halves(acc)
        top_ref[0, b] = jnp.broadcast_to(top, top_ref.shape[2:])
        sum_ref[0, b] = jnp.broadcast_to(total, sum_ref.shape[2:])


def far_kernel(qt_ref, k_ref, vt_ref, acc_ref, top_ref, sum_ref, out_ref):
    f32 = jnp.float32
    spread = RAND * BLK
    shared = slice(2 * spread, 2 * spread + BLK)
    scores = []
    for b in range(2):
        q = both_heads(qt_ref[:, b * BLK : (b + 1) * BLK])
        keys = k_ref[b * spread : (b + 1) * spread, :]
        s = jnp.dot(keys, q, preferred_element_type=f32)
        scores.append((s, jnp.dot(k_ref[shared, :], q, preferred_element_type=f32)))
    for b, (s, g) in enumerate(scores):
        cols = slice(b * BLK, (b + 1) * BLK)
        far = slice(b * spread, (b + 1) * spread)
        old_top = top_ref[0, b, :1]
        top = jnp.maximum(jnp.max(s, axis=0, keepdims=True), old_top)
        top = jnp.maximum(jnp.max(g, axis=0, keepdims=True), top)
        p = jnp.exp(s - top)
        pg = jnp.exp(g - top)
        scale = jnp.exp(old_top - top)
        total = jnp.sum(p, axis=0, keepdims=True) + sum_ref[0, b, :1] * scale
        total += jnp.sum(pg, axis=0, keepdims=True)
        acc = jnp.dot(vt_ref[:, far], p.astype(jnp.bfloat16), preferred_element_type=f32)
        acc += jnp.dot(vt_ref[:, shared], pg.astype(jnp.bfloat16), preferred_element_type=f32)
        half = acc.shape[0] // 2
        acc = own_halves(acc) + acc_ref[:, cols] * spread_rows(scale, half)
        out_ref[:, cols] = (acc / spread_rows(total, half)).astype(jnp.bfloat16)


def pair_specs(rows, keys):
    tall = pl.BlockSpec((BLK, rows), lambda i: (i, 0))
    k_spec = pl.BlockSpec((keys, BLK), lambda i: (0, i))
    vt_spec = pl.BlockSpec((BLK, keys), lambda i: (i, 0))
    row = pl.BlockSpec((1, rows // BLK, 8, 2 * BLK), lambda i: (i, 0, 0, 0))
    return tall, k_spec, vt_spec, row


def near_attention(qt, k, vt, mask):
    width, rows = qt.shape
    pairs = width // BLK
    tall, k_spec, vt_spec, row = pair_specs(rows, k.shape[0])
    stat = jax.ShapeDtypeStruct((pairs, rows // BLK, 8, 2 * BLK), jnp.float32)
    return pl.pallas_call(
        near_kernel,
        out_shape=(jax.ShapeDtypeStruct((width, rows), jnp.float32), stat, stat),
        grid=(pairs,),
        in_specs=[tall, k_spec, vt_spec, pl.BlockSpec(mask.shape, lambda i: (0, 0, 0))],
        out_specs=(tall, row, row),
        name="near_attention",
    )(qt, k, vt, mask)


def far_attention(qt, k, vt, parts):
    width, rows = qt.shape
    tall, k_spec, vt_spec, row = pair_specs(rows, k.shape[0])
    return pl.pallas_call(
        far_kernel,
        out_shape=jax.ShapeDtypeStruct((width, rows), jnp.bfloat16),
        grid=(width // BLK,),
        in_specs=[tall, k_spec, vt_spec, tall, row, row],
        out_specs=tall,
        name="far_attention",
    )(qt, k, vt, *parts)


def run_copies(copies):
    for copy in copies:
        copy.start()
    for copy in copies:
        copy.wait()


def piece_kernel(core_ref, wt_ref, out_w_ref, piece_ref, sems):
    rows, cols = wt_ref.shape[0], piece_ref.shape[1]
    mine = pl.ds(pl.multiple_of(core_ref[0] * cols, cols), cols)
    run_copies(
        [
            pltpu.make_async_copy(wt_ref.at[:, mine], piece_ref.at[:rows], sems.at[0]),
            pltpu.make_async_copy(out_w_ref.at[:, mine], piece_ref.at[rows:], sems.at[1]),
        ]
    )


def any_specs(count):
    return [pl.BlockSpec(memory_space=pl.ANY)] * count


def own_piece(core, wt, out_w):
    rows = wt.shape[0] + out_w.shape[0]
    return pl.pallas_call(
        piece_kernel,
        out_shape=jax.ShapeDtypeStruct((rows, wt.shape[1] // 2), jnp.bfloat16),
        in_specs=[pl.BlockSpec(memory_space=pltpu.SMEM)] + any_specs(2),
        out_specs=pl.BlockSpec(memory_space=pltpu.VMEM),
        scratch_shapes=[pltpu.SemaphoreType.DMA((2,))],
        name="own_piece",
    )(core, wt, out_w)


def assemble_kernel(core_ref, *refs):
    sems = refs[-1]
    outs, parts = refs[-5:-1], refs[:-5]
    heads, hd, width = outs[0].shape
    cols = width // 2
    copies, head = [], 0
    for n, part in enumerate(parts):
        side = core_ref[0] if head < heads else 1 - core_ref[0]
        into_cols = pl.ds(pl.multiple_of(side * cols, cols), cols)
        count = part.shape[0]
        into_heads = pl.ds(head % heads, count)
        head += count
        for k, out in enumerate(outs):
            copies.append(
                pltpu.make_async_copy(
                    part.at[:, pl.ds(k * hd, hd)],
                    out.at[into_heads, :, into_cols],
                    sems.at[n * len(outs) + k],
                )
            )
    run_copies(copies)


def assemble(core, parts, heads, hd):
    cols = parts[0].shape[2]
    one = jax.ShapeDtypeStruct((heads, hd, 2 * cols), jnp.bfloat16)
    return pl.pallas_call(
        assemble_kernel,
        out_shape=(one,) * 4,
        in_specs=[pl.BlockSpec(memory_space=pltpu.SMEM)] + any_specs(len(parts)),
        out_specs=(pl.BlockSpec(memory_space=pltpu.VMEM),) * 4,
        scratch_shapes=[pltpu.SemaphoreType.DMA((4 * len(parts),))],
        name="assemble",
    )(core, *parts)


def tied(value, *others):
    return lax.optimization_barrier((value,) + others)[0]


def swap(value, bits, devices):
    return lax.ppermute(value, ("ctx", "head"), [(i, i ^ bits) for i in range(devices)])


def exchange_plan(pairs_dev, pairs_off, ctx_count, ctx_index, lower):
    pair_count = lower.shape[0]
    all_dev = pairs_dev.reshape(ctx_count, pair_count)
    all_off = pairs_off.reshape(ctx_count, pair_count)
    own = all_dev == ctx_index
    rank = jnp.sum((own[:, None, :] & lower[None]).astype(jnp.int32), axis=2)
    slot = jnp.arange(CAP, dtype=jnp.int32)
    chosen = own[:, None, :] & (rank[:, None, :] == slot[None, :, None])
    send = jnp.sum(jnp.where(chosen, all_off[:, None, :], 0), axis=2)
    send = send.reshape(-1)
    own_dev = lax.dynamic_index_in_dim(all_dev, ctx_index, 0, keepdims=False)
    earlier = (own_dev[:, None] == own_dev[None, :]) & lower
    take = own_dev * CAP + jnp.sum(earlier.astype(jnp.int32), axis=1)
    return send, take


def window_mask(lengths, first_pos, doc_tokens, rows):
    line_end = jnp.cumsum(lengths)
    positions = first_pos - BLK + jnp.arange(rows + 2 * BLK, dtype=jnp.int32)
    line = jnp.sum((line_end[None, :] <= positions[:, None]).astype(jnp.int32), axis=1)
    inside = (positions >= 0) & (positions < doc_tokens)
    line = jnp.where(inside, line, -1)
    masks = []
    for b in range(rows // BLK):
        keys = line[b * BLK : (b + 3) * BLK]
        queries = line[(b + 1) * BLK : (b + 2) * BLK]
        masks.append(jnp.where(keys[:, None] == queries[None, :], 0.0, NEG))
    return jnp.stack(masks).astype(jnp.float32)


def per_device(
    tokens, ln_gain, ln_bias, qkv_weight, out_weight, out_bias, lengths, pairs_dev, pairs_off
):
    ctx_count = lax.axis_size("ctx")
    heads = lax.axis_size("head")
    devices = ctx_count * heads
    ctx_index = lax.axis_index("ctx")
    head_index = lax.axis_index("head")
    rows, width = tokens.shape
    hd = width // heads

    wt = jnp.transpose(qkv_weight[:, 0, :])
    core = (ctx_index % 2).astype(jnp.int32).reshape(1)
    place = ctx_index * heads + head_index

    normed_t, first, last = layer_norm(tokens, ln_gain, ln_bias, heads)
    cells = lax.all_to_all(normed_t, "head", split_axis=0, concat_axis=0, tiled=True)

    own = own_piece(core, wt, out_weight)
    along_y = [list(range(first_x, heads, 2)) for first_x in range(2)]
    column = lax.all_gather(own, "head", axis_index_groups=along_y)

    both = ("ctx", "head")
    right = [(i, i + 1) for i in range(devices - 1)]
    left = [(i + 1, i) for i in range(devices - 1)]
    before = lax.ppermute(last, both, right)
    after = lax.ppermute(first, both, left)

    pair_count = (heads * rows // BLK) * RAND
    order = jnp.arange(pair_count, dtype=jnp.int32)
    lower = order[None, :] < order[:, None]
    send, take = exchange_plan(pairs_dev, pairs_off, ctx_count, ctx_index, lower)
    outgoing = pick_blocks(tied(send, own, before, after), cells)
    outgoing = outgoing.reshape(ctx_count, CAP * hd, BLK)
    slots = lax.all_to_all(outgoing, "ctx", split_axis=0, concat_axis=0, tiled=True)
    slots = slots.reshape(ctx_count * CAP, hd, BLK)

    half = column.shape[0] // 2
    mine = [column, swap(column[:half], 1, devices), swap(column[half:], 2 * heads + 1, devices)]
    other = [swap(part, heads, devices) for part in mine]
    shared = jnp.where(ctx_index == 0, cells[0, :, :BLK], 0).astype(jnp.bfloat16)
    reach = 1
    while reach < ctx_count:
        hop = [(i, i + reach) for i in range(reach)]
        shared = shared + lax.ppermute(shared, "ctx", hop)
        reach *= 2
    placed = place_blocks(tied(take, column), slots, shared, heads)
    far = lax.all_to_all(placed, "head", split_axis=0, concat_axis=0, tiled=True)
    far = far.reshape(width, far.shape[2])

    near = jnp.concatenate([before, normed_t, after], axis=2)
    near = near.reshape(width, near.shape[2])

    mask = window_mask(lengths, place * rows, devices * rows, rows)

    f32 = jnp.float32
    bf16 = jnp.bfloat16
    weights = assemble(core, mine + other, heads, hd)
    w_q, w_k, w_v, w_o = (w.reshape(width, width) for w in weights)
    own_t = normed_t.reshape(width, rows)
    qt = jnp.dot(w_q, own_t, preferred_element_type=f32).astype(bf16)
    qt = (qt.astype(f32) * hd**-0.5).astype(bf16)
    k_near = lax.dot_general(near, w_k, TN, preferred_element_type=f32).astype(bf16)
    vt_near = jnp.dot(w_v, near, preferred_element_type=f32).astype(bf16)
    parts = near_attention(qt, k_near, vt_near, mask)
    k_far = lax.dot_general(far, w_k, TN, preferred_element_type=f32).astype(bf16)
    vt_far = jnp.dot(w_v, far, preferred_element_type=f32).astype(bf16)
    attended = far_attention(qt, k_far, vt_far, parts)
    projected = lax.dot_general(
        attended, w_o, (((0,), (0,)), ((), ())), preferred_element_type=f32
    )
    return (projected + out_bias).astype(bf16)


def solution(mesh):
    in_specs = (
        P(("ctx", "head"), None),
        P(),
        P(),
        P(None, "head", None),
        P("head", None),
        P(),
        P(),
        P(),
        P(),
    )

    return jax.shard_map(
        per_device,
        mesh=mesh,
        in_specs=in_specs,
        out_specs=P(("ctx", "head"), None),
        check_vma=False,
    )
```

```python
import jax
import jax.numpy as jnp
from jax import lax
from jax.experimental import pallas as pl
from jax.experimental.pallas import tpu as pltpu
from jax.sharding import PartitionSpec as P


BLK = 128
RAND = 3
CAP = 4
EPS = 1e-05
NEG = float("-inf")
TN = (((0,), (1,)), ((), ()))


def ln_kernel(tok_ref, gain_ref, bias_ref, normt_ref, first_ref, last_ref):
    values = tok_ref[...].astype(jnp.float32)
    center = values - jnp.mean(values, axis=-1, keepdims=True)
    spread = jnp.mean(center * center, axis=-1, keepdims=True)
    normed = center * lax.rsqrt(spread + EPS) * gain_ref[...] + bias_ref[...]
    turned = jnp.transpose(normed).astype(jnp.bfloat16).reshape(normt_ref.shape)
    normt_ref[...] = turned
    first_ref[...] = turned[:, :, :BLK]
    last_ref[...] = turned[:, :, turned.shape[2] - BLK :]


def layer_norm(tokens, gain, bias, heads):
    rows, width = tokens.shape
    return pl.pallas_call(
        ln_kernel,
        out_shape=tuple(
            jax.ShapeDtypeStruct((heads, width // heads, cols), jnp.bfloat16)
            for cols in (rows, BLK, BLK)
        ),
        name="layer_norm",
    )(tokens, gain.reshape(1, width), bias.reshape(1, width))


def pick_kernel(ids_ref, cells_ref, out_ref):
    def step(slot, carry):
        block = ids_ref[slot]
        cols = pl.ds(pl.multiple_of((block % 2) * BLK, BLK), BLK)
        out_ref[slot] = cells_ref[block // 2, :, cols]
        return carry

    lax.fori_loop(0, out_ref.shape[0], step, 0, unroll=4)


def pick_blocks(ids, cells):
    return pl.pallas_call(
        pick_kernel,
        out_shape=jax.ShapeDtypeStruct((ids.shape[0], cells.shape[1], BLK), jnp.bfloat16),
        in_specs=[
            pl.BlockSpec(memory_space=pltpu.SMEM),
            pl.BlockSpec(memory_space=pltpu.VMEM),
        ],
        out_specs=pl.BlockSpec(memory_space=pltpu.VMEM),
        name="pick_blocks",
    )(ids, cells)


def place_kernel(pos_ref, slots_ref, shared_ref, out_ref):
    per_dev = out_ref.shape[2] // BLK - 1

    def step(dev, carry):
        for j in range(per_dev):
            out_ref[dev, :, j * BLK : (j + 1) * BLK] = slots_ref[pos_ref[dev * per_dev + j]]
        out_ref[dev, :, per_dev * BLK :] = shared_ref[...]
        return carry

    lax.fori_loop(0, out_ref.shape[0], step, 0)


def place_blocks(pos, slots, shared, heads):
    cols = (pos.shape[0] // heads + 1) * BLK
    return pl.pallas_call(
        place_kernel,
        out_shape=jax.ShapeDtypeStruct((heads, slots.shape[1], cols), jnp.bfloat16),
        in_specs=[
            pl.BlockSpec(memory_space=pltpu.SMEM),
            pl.BlockSpec(memory_space=pltpu.VMEM),
            pl.BlockSpec(memory_space=pltpu.VMEM),
        ],
        out_specs=pl.BlockSpec(memory_space=pltpu.VMEM),
        name="place_blocks",
    )(pos, slots, shared)


def both_heads(qt_pair):
    half = qt_pair.shape[0] // 2
    none = jnp.zeros((half, qt_pair.shape[1]), qt_pair.dtype)
    top = jnp.concatenate([qt_pair[:half], none], axis=1)
    return jnp.concatenate([top, jnp.concatenate([none, qt_pair[half:]], axis=1)], axis=0)


def own_halves(wide):
    half, cols = wide.shape[0] // 2, wide.shape[1] // 2
    return jnp.concatenate([wide[:half, :cols], wide[half:, cols:]], axis=0)


def spread_rows(row, half):
    cols = row.shape[1] // 2
    top = jnp.broadcast_to(row[:, :cols], (half, cols))
    return jnp.concatenate([top, jnp.broadcast_to(row[:, cols:], (half, cols))], axis=0)


def near_kernel(qt_ref, k_ref, vt_ref, mask_ref, acc_ref, top_ref, sum_ref):
    f32 = jnp.float32
    scores = []
    for b in range(2):
        q = both_heads(qt_ref[:, b * BLK : (b + 1) * BLK])
        keys = k_ref[b * BLK : (b + 3) * BLK, :]
        mask = mask_ref[b]
        s = jnp.dot(keys, q, preferred_element_type=f32)
        scores.append(s + jnp.concatenate([mask, mask], axis=1))
    for b, s in enumerate(scores):
        top = jnp.max(s, axis=0, keepdims=True)
        p = jnp.exp(s - top)
        total = jnp.sum(p, axis=0, keepdims=True)
        near = slice(b * BLK, (b + 3) * BLK)
        acc = jnp.dot(vt_ref[:, near], p.astype(jnp.bfloat16), preferred_element_type=f32)
        acc_ref[:, b * BLK : (b + 1) * BLK] = own_halves(acc)
        top_ref[0, b] = jnp.broadcast_to(top, top_ref.shape[2:])
        sum_ref[0, b] = jnp.broadcast_to(total, sum_ref.shape[2:])


def far_kernel(qt_ref, k_ref, vt_ref, acc_ref, top_ref, sum_ref, out_ref):
    f32 = jnp.float32
    spread = RAND * BLK
    shared = slice(2 * spread, 2 * spread + BLK)
    scores = []
    for b in range(2):
        q = both_heads(qt_ref[:, b * BLK : (b + 1) * BLK])
        keys = k_ref[b * spread : (b + 1) * spread, :]
        s = jnp.dot(keys, q, preferred_element_type=f32)
        scores.append((s, jnp.dot(k_ref[shared, :], q, preferred_element_type=f32)))
    for b, (s, g) in enumerate(scores):
        cols = slice(b * BLK, (b + 1) * BLK)
        far = slice(b * spread, (b + 1) * spread)
        old_top = top_ref[0, b, :1]
        top = jnp.maximum(jnp.max(s, axis=0, keepdims=True), old_top)
        top = jnp.maximum(jnp.max(g, axis=0, keepdims=True), top)
        p = jnp.exp(s - top)
        pg = jnp.exp(g - top)
        scale = jnp.exp(old_top - top)
        total = jnp.sum(p, axis=0, keepdims=True) + sum_ref[0, b, :1] * scale
        total += jnp.sum(pg, axis=0, keepdims=True)
        acc = jnp.dot(vt_ref[:, far], p.astype(jnp.bfloat16), preferred_element_type=f32)
        acc += jnp.dot(vt_ref[:, shared], pg.astype(jnp.bfloat16), preferred_element_type=f32)
        half = acc.shape[0] // 2
        acc = own_halves(acc) + acc_ref[:, cols] * spread_rows(scale, half)
        out_ref[:, cols] = (acc / spread_rows(total, half)).astype(jnp.bfloat16)


def pair_specs(rows, keys):
    tall = pl.BlockSpec((BLK, rows), lambda i: (i, 0))
    k_spec = pl.BlockSpec((keys, BLK), lambda i: (0, i))
    vt_spec = pl.BlockSpec((BLK, keys), lambda i: (i, 0))
    row = pl.BlockSpec((1, rows // BLK, 8, 2 * BLK), lambda i: (i, 0, 0, 0))
    return tall, k_spec, vt_spec, row


def near_attention(qt, k, vt, mask):
    width, rows = qt.shape
    pairs = width // BLK
    tall, k_spec, vt_spec, row = pair_specs(rows, k.shape[0])
    stat = jax.ShapeDtypeStruct((pairs, rows // BLK, 8, 2 * BLK), jnp.float32)
    return pl.pallas_call(
        near_kernel,
        out_shape=(jax.ShapeDtypeStruct((width, rows), jnp.float32), stat, stat),
        grid=(pairs,),
        in_specs=[tall, k_spec, vt_spec, pl.BlockSpec(mask.shape, lambda i: (0, 0, 0))],
        out_specs=(tall, row, row),
        name="near_attention",
    )(qt, k, vt, mask)


def far_attention(qt, k, vt, parts):
    width, rows = qt.shape
    tall, k_spec, vt_spec, row = pair_specs(rows, k.shape[0])
    return pl.pallas_call(
        far_kernel,
        out_shape=jax.ShapeDtypeStruct((width, rows), jnp.bfloat16),
        grid=(width // BLK,),
        in_specs=[tall, k_spec, vt_spec, tall, row, row],
        out_specs=tall,
        name="far_attention",
    )(qt, k, vt, *parts)


def run_copies(copies):
    for copy in copies:
        copy.start()
    for copy in copies:
        copy.wait()


def piece_kernel(core_ref, wt_ref, out_w_ref, piece_ref, sems):
    rows, cols = wt_ref.shape[0], piece_ref.shape[1]
    mine = pl.ds(pl.multiple_of(core_ref[0] * cols, cols), cols)
    run_copies(
        [
            pltpu.make_async_copy(wt_ref.at[:, mine], piece_ref.at[:rows], sems.at[0]),
            pltpu.make_async_copy(out_w_ref.at[:, mine], piece_ref.at[rows:], sems.at[1]),
        ]
    )


def any_specs(count):
    return [pl.BlockSpec(memory_space=pl.ANY)] * count


def own_piece(core, wt, out_w):
    rows = wt.shape[0] + out_w.shape[0]
    return pl.pallas_call(
        piece_kernel,
        out_shape=jax.ShapeDtypeStruct((rows, wt.shape[1] // 2), jnp.bfloat16),
        in_specs=[pl.BlockSpec(memory_space=pltpu.SMEM)] + any_specs(2),
        out_specs=pl.BlockSpec(memory_space=pltpu.VMEM),
        scratch_shapes=[pltpu.SemaphoreType.DMA((2,))],
        name="own_piece",
    )(core, wt, out_w)


def assemble_kernel(core_ref, *refs):
    sems = refs[-1]
    outs, parts = refs[-5:-1], refs[:-5]
    heads, hd, width = outs[0].shape
    cols = width // 2
    copies, head = [], 0
    for n, part in enumerate(parts):
        side = core_ref[0] if head < heads else 1 - core_ref[0]
        into_cols = pl.ds(pl.multiple_of(side * cols, cols), cols)
        count = part.shape[0]
        into_heads = pl.ds(head % heads, count)
        head += count
        for k, out in enumerate(outs):
            copies.append(
                pltpu.make_async_copy(
                    part.at[:, pl.ds(k * hd, hd)],
                    out.at[into_heads, :, into_cols],
                    sems.at[n * len(outs) + k],
                )
            )
    run_copies(copies)


def assemble(core, parts, heads, hd):
    cols = parts[0].shape[2]
    one = jax.ShapeDtypeStruct((heads, hd, 2 * cols), jnp.bfloat16)
    return pl.pallas_call(
        assemble_kernel,
        out_shape=(one,) * 4,
        in_specs=[pl.BlockSpec(memory_space=pltpu.SMEM)] + any_specs(len(parts)),
        out_specs=(pl.BlockSpec(memory_space=pltpu.VMEM),) * 4,
        scratch_shapes=[pltpu.SemaphoreType.DMA((4 * len(parts),))],
        name="assemble",
    )(core, *parts)


def tied(value, *others):
    return lax.optimization_barrier((value,) + others)[0]


def swap(value, bits, devices):
    return lax.ppermute(value, ("ctx", "head"), [(i, i ^ bits) for i in range(devices)])


def exchange_plan(pairs_dev, pairs_off, ctx_count, ctx_index, lower):
    pair_count = lower.shape[0]
    all_dev = pairs_dev.reshape(ctx_count, pair_count)
    all_off = pairs_off.reshape(ctx_count, pair_count)
    own = all_dev == ctx_index
    rank = jnp.sum((own[:, None, :] & lower[None]).astype(jnp.int32), axis=2)
    slot = jnp.arange(CAP, dtype=jnp.int32)
    chosen = own[:, None, :] & (rank[:, None, :] == slot[None, :, None])
    send = jnp.sum(jnp.where(chosen, all_off[:, None, :], 0), axis=2)
    send = send.reshape(-1)
    own_dev = lax.dynamic_index_in_dim(all_dev, ctx_index, 0, keepdims=False)
    earlier = (own_dev[:, None] == own_dev[None, :]) & lower
    take = own_dev * CAP + jnp.sum(earlier.astype(jnp.int32), axis=1)
    return send, take


def window_mask(lengths, first_pos, doc_tokens, rows):
    line_end = jnp.cumsum(lengths)
    positions = first_pos - BLK + jnp.arange(rows + 2 * BLK, dtype=jnp.int32)
    line = jnp.sum((line_end[None, :] <= positions[:, None]).astype(jnp.int32), axis=1)
    inside = (positions >= 0) & (positions < doc_tokens)
    line = jnp.where(inside, line, -1)
    masks = []
    for b in range(rows // BLK):
        keys = line[b * BLK : (b + 3) * BLK]
        queries = line[(b + 1) * BLK : (b + 2) * BLK]
        masks.append(jnp.where(keys[:, None] == queries[None, :], 0.0, NEG))
    return jnp.stack(masks).astype(jnp.float32)


def per_device(
    tokens, ln_gain, ln_bias, qkv_weight, out_weight, out_bias, lengths, pairs_dev, pairs_off
):
    ctx_count = lax.axis_size("ctx")
    heads = lax.axis_size("head")
    devices = ctx_count * heads
    ctx_index = lax.axis_index("ctx")
    head_index = lax.axis_index("head")
    rows, width = tokens.shape
    hd = width // heads

    wt = jnp.transpose(qkv_weight[:, 0, :])
    core = (ctx_index % 2).astype(jnp.int32).reshape(1)
    place = ctx_index * heads + head_index

    normed_t, first, last = layer_norm(tokens, ln_gain, ln_bias, heads)
    cells = lax.all_to_all(normed_t, "head", split_axis=0, concat_axis=0, tiled=True)

    own = own_piece(core, wt, out_weight)
    along_y = [list(range(first_x, heads, 2)) for first_x in range(2)]
    column = lax.all_gather(own, "head", axis_index_groups=along_y)

    both = ("ctx", "head")
    right = [(i, i + 1) for i in range(devices - 1)]
    left = [(i + 1, i) for i in range(devices - 1)]
    before = lax.ppermute(tied(last, cells), both, right)
    after = lax.ppermute(tied(first, cells), both, left)

    pair_count = (heads * rows // BLK) * RAND
    order = jnp.arange(pair_count, dtype=jnp.int32)
    lower = order[None, :] < order[:, None]
    send, take = exchange_plan(pairs_dev, pairs_off, ctx_count, ctx_index, lower)
    outgoing = pick_blocks(tied(send, own), cells)
    outgoing = outgoing.reshape(ctx_count, CAP * hd, BLK)
    slots = lax.all_to_all(outgoing, "ctx", split_axis=0, concat_axis=0, tiled=True)
    slots = slots.reshape(ctx_count * CAP, hd, BLK)

    half = column.shape[0] // 2
    mine = [column, swap(column[:half], 1, devices), swap(column[half:], 2 * heads + 1, devices)]
    other = [swap(part, heads, devices) for part in mine]
    shared = jnp.where(ctx_index == 0, cells[0, :, :BLK], 0).astype(jnp.bfloat16)
    group = 4
    for reach in (1, 2):
        hop = [(i, i + reach) for i in range(reach)]
        shared = shared + lax.ppermute(shared, "ctx", hop)
    copies = [
        lax.ppermute(shared, "ctx", [(i, i + reach) for i in range(group)])
        for reach in range(group, ctx_count, group)
    ]
    for copy in copies:
        shared = shared + copy
    placed = place_blocks(tied(take, column, before, after), slots, shared, heads)
    far = lax.all_to_all(placed, "head", split_axis=0, concat_axis=0, tiled=True)
    far = far.reshape(width, far.shape[2])

    near = jnp.concatenate([before, normed_t, after], axis=2)
    near = near.reshape(width, near.shape[2])

    mask = window_mask(lengths, place * rows, devices * rows, rows)

    f32 = jnp.float32
    bf16 = jnp.bfloat16
    weights = assemble(core, mine + other, heads, hd)
    w_q, w_k, w_v, w_o = (w.reshape(width, width) for w in weights)
    own_t = normed_t.reshape(width, rows)
    qt = jnp.dot(w_q, own_t, preferred_element_type=f32).astype(bf16)
    qt = (qt.astype(f32) * hd**-0.5).astype(bf16)
    k_near = lax.dot_general(near, w_k, TN, preferred_element_type=f32).astype(bf16)
    vt_near = jnp.dot(w_v, near, preferred_element_type=f32).astype(bf16)
    parts = near_attention(qt, k_near, vt_near, mask)
    k_far = lax.dot_general(far, w_k, TN, preferred_element_type=f32).astype(bf16)
    vt_far = jnp.dot(w_v, far, preferred_element_type=f32).astype(bf16)
    attended = far_attention(qt, k_far, vt_far, parts)
    projected = lax.dot_general(
        attended, w_o, (((0,), (0,)), ((), ())), preferred_element_type=f32
    )
    return (projected + out_bias).astype(bf16)


def solution(mesh):
    in_specs = (
        P(("ctx", "head"), None),
        P(),
        P(),
        P(None, "head", None),
        P("head", None),
        P(),
        P(),
        P(),
        P(),
    )

    return jax.shard_map(
        per_device,
        mesh=mesh,
        in_specs=in_specs,
        out_specs=P(("ctx", "head"), None),
        check_vma=False,
    )
```

```python
import jax
import jax.numpy as jnp
from jax import lax
from jax.experimental import pallas as pl
from jax.experimental.pallas import tpu as pltpu
from jax.sharding import PartitionSpec as P


BLK = 128
RAND = 3
CAP = 4
EPS = 1e-05
NEG = float("-inf")
TN = (((0,), (1,)), ((), ()))
BOTH_FIRST = (((0,), (0,)), ((), ()))


def ln_kernel(tok_ref, gain_ref, bias_ref, normt_ref, first_ref, last_ref):
    values = tok_ref[...].astype(jnp.float32)
    center = values - jnp.mean(values, axis=-1, keepdims=True)
    spread = jnp.mean(center * center, axis=-1, keepdims=True)
    normed = center * lax.rsqrt(spread + EPS) * gain_ref[...] + bias_ref[...]
    turned = jnp.transpose(normed).astype(jnp.bfloat16).reshape(normt_ref.shape)
    normt_ref[...] = turned
    first_ref[...] = turned[:, :, :BLK]
    last_ref[...] = turned[:, :, turned.shape[2] - BLK :]


def layer_norm(tokens, gain, bias, heads):
    rows, width = tokens.shape
    return pl.pallas_call(
        ln_kernel,
        out_shape=tuple(
            jax.ShapeDtypeStruct((heads, width // heads, cols), jnp.bfloat16)
            for cols in (rows, BLK, BLK)
        ),
        name="layer_norm",
    )(tokens, gain.reshape(1, width), bias.reshape(1, width))


def pick_kernel(ids_ref, cells_ref, out_ref):
    def step(slot, carry):
        block = ids_ref[slot]
        cols = pl.ds(pl.multiple_of((block % 2) * BLK, BLK), BLK)
        out_ref[slot] = cells_ref[block // 2, :, cols]
        return carry

    lax.fori_loop(0, out_ref.shape[0], step, 0, unroll=4)


def pick_blocks(ids, cells):
    return pl.pallas_call(
        pick_kernel,
        out_shape=jax.ShapeDtypeStruct((ids.shape[0], cells.shape[1], BLK), jnp.bfloat16),
        in_specs=[
            pl.BlockSpec(memory_space=pltpu.SMEM),
            pl.BlockSpec(memory_space=pltpu.VMEM),
        ],
        out_specs=pl.BlockSpec(memory_space=pltpu.VMEM),
        name="pick_blocks",
    )(ids, cells)


def place_kernel(pos_ref, slots_ref, shared_ref, out_ref):
    per_dev = out_ref.shape[2] // BLK - 1

    def step(dev, carry):
        for j in range(per_dev):
            out_ref[dev, :, j * BLK : (j + 1) * BLK] = slots_ref[pos_ref[dev * per_dev + j]]
        out_ref[dev, :, per_dev * BLK :] = shared_ref[...]
        return carry

    lax.fori_loop(0, out_ref.shape[0], step, 0)


def place_blocks(pos, slots, shared, heads):
    cols = (pos.shape[0] // heads + 1) * BLK
    return pl.pallas_call(
        place_kernel,
        out_shape=jax.ShapeDtypeStruct((heads, slots.shape[1], cols), jnp.bfloat16),
        in_specs=[
            pl.BlockSpec(memory_space=pltpu.SMEM),
            pl.BlockSpec(memory_space=pltpu.VMEM),
            pl.BlockSpec(memory_space=pltpu.VMEM),
        ],
        out_specs=pl.BlockSpec(memory_space=pltpu.VMEM),
        name="place_blocks",
    )(pos, slots, shared)


def both_heads(qt_pair):
    half = qt_pair.shape[0] // 2
    none = jnp.zeros((half, qt_pair.shape[1]), qt_pair.dtype)
    top = jnp.concatenate([qt_pair[:half], none], axis=1)
    return jnp.concatenate([top, jnp.concatenate([none, qt_pair[half:]], axis=1)], axis=0)


def own_halves(wide):
    half, cols = wide.shape[0] // 2, wide.shape[1] // 2
    return jnp.concatenate([wide[:half, :cols], wide[half:, cols:]], axis=0)


def spread_rows(row, half):
    cols = row.shape[1] // 2
    top = jnp.broadcast_to(row[:, :cols], (half, cols))
    return jnp.concatenate([top, jnp.broadcast_to(row[:, cols:], (half, cols))], axis=0)


def near_kernel(qt_ref, k_ref, vt_ref, mask_ref, acc_ref, top_ref, sum_ref):
    f32 = jnp.float32
    scores = []
    for b in range(2):
        q = both_heads(qt_ref[:, b * BLK : (b + 1) * BLK])
        keys = k_ref[b * BLK : (b + 3) * BLK, :]
        mask = mask_ref[b]
        s = jnp.dot(keys, q, preferred_element_type=f32)
        scores.append(s + jnp.concatenate([mask, mask], axis=1))
    for b, s in enumerate(scores):
        top = jnp.max(s, axis=0, keepdims=True)
        p = jnp.exp(s - top)
        total = jnp.sum(p, axis=0, keepdims=True)
        near = slice(b * BLK, (b + 3) * BLK)
        acc = jnp.dot(vt_ref[:, near], p.astype(jnp.bfloat16), preferred_element_type=f32)
        acc_ref[:, b * BLK : (b + 1) * BLK] = own_halves(acc)
        top_ref[0, b] = jnp.broadcast_to(top, top_ref.shape[2:])
        sum_ref[0, b] = jnp.broadcast_to(total, sum_ref.shape[2:])


def far_kernel(qt_ref, wk_ref, wv_ref, x_ref, acc_ref, top_ref, sum_ref, out_ref):
    f32 = jnp.float32
    kt = jnp.dot(wk_ref[...], x_ref[...], preferred_element_type=f32).astype(jnp.bfloat16)
    vt = jnp.dot(wv_ref[...], x_ref[...], preferred_element_type=f32).astype(jnp.bfloat16)
    spread = RAND * BLK
    shared = slice(2 * spread, 2 * spread + BLK)
    scores = []
    for b in range(2):
        q = both_heads(qt_ref[:, b * BLK : (b + 1) * BLK])
        keys = kt[:, b * spread : (b + 1) * spread]
        s = lax.dot_general(keys, q, BOTH_FIRST, preferred_element_type=f32)
        g = lax.dot_general(kt[:, shared], q, BOTH_FIRST, preferred_element_type=f32)
        scores.append((s, g))
    for b, (s, g) in enumerate(scores):
        cols = slice(b * BLK, (b + 1) * BLK)
        far = slice(b * spread, (b + 1) * spread)
        old_top = top_ref[0, b, :1]
        top = jnp.maximum(jnp.max(s, axis=0, keepdims=True), old_top)
        top = jnp.maximum(jnp.max(g, axis=0, keepdims=True), top)
        p = jnp.exp(s - top)
        pg = jnp.exp(g - top)
        scale = jnp.exp(old_top - top)
        total = jnp.sum(p, axis=0, keepdims=True) + sum_ref[0, b, :1] * scale
        total += jnp.sum(pg, axis=0, keepdims=True)
        acc = jnp.dot(vt[:, far], p.astype(jnp.bfloat16), preferred_element_type=f32)
        acc += jnp.dot(vt[:, shared], pg.astype(jnp.bfloat16), preferred_element_type=f32)
        half = acc.shape[0] // 2
        acc = own_halves(acc) + acc_ref[:, cols] * spread_rows(scale, half)
        out_ref[:, cols] = (acc / spread_rows(total, half)).astype(jnp.bfloat16)


def pair_specs(rows, keys):
    tall = pl.BlockSpec((BLK, rows), lambda i: (i, 0))
    k_spec = pl.BlockSpec((keys, BLK), lambda i: (0, i))
    vt_spec = pl.BlockSpec((BLK, keys), lambda i: (i, 0))
    row = pl.BlockSpec((1, rows // BLK, 8, 2 * BLK), lambda i: (i, 0, 0, 0))
    return tall, k_spec, vt_spec, row


def near_attention(qt, k, vt, mask):
    width, rows = qt.shape
    pairs = width // BLK
    tall, k_spec, vt_spec, row = pair_specs(rows, k.shape[0])
    stat = jax.ShapeDtypeStruct((pairs, rows // BLK, 8, 2 * BLK), jnp.float32)
    return pl.pallas_call(
        near_kernel,
        out_shape=(jax.ShapeDtypeStruct((width, rows), jnp.float32), stat, stat),
        grid=(pairs,),
        in_specs=[tall, k_spec, vt_spec, pl.BlockSpec(mask.shape, lambda i: (0, 0, 0))],
        out_specs=(tall, row, row),
        name="near_attention",
    )(qt, k, vt, mask)


def far_attention(qt, w_k, w_v, x, parts):
    width, rows = qt.shape
    tall, _, _, row = pair_specs(rows, x.shape[1])
    weight = pl.BlockSpec((BLK, width), lambda i: (i, 0))
    whole = pl.BlockSpec(x.shape, lambda i: (0, 0))
    return pl.pallas_call(
        far_kernel,
        out_shape=jax.ShapeDtypeStruct((width, rows), jnp.bfloat16),
        grid=(width // BLK,),
        in_specs=[tall, weight, weight, whole, tall, row, row],
        out_specs=tall,
        name="far_attention",
    )(qt, w_k, w_v, x, *parts)


def run_copies(copies):
    for copy in copies:
        copy.start()
    for copy in copies:
        copy.wait()


def piece_kernel(core_ref, wt_ref, out_w_ref, piece_ref, sems):
    rows, cols = wt_ref.shape[0], piece_ref.shape[1]
    mine = pl.ds(pl.multiple_of(core_ref[0] * cols, cols), cols)
    run_copies(
        [
            pltpu.make_async_copy(wt_ref.at[:, mine], piece_ref.at[:rows], sems.at[0]),
            pltpu.make_async_copy(out_w_ref.at[:, mine], piece_ref.at[rows:], sems.at[1]),
        ]
    )


def any_specs(count):
    return [pl.BlockSpec(memory_space=pl.ANY)] * count


def own_piece(core, wt, out_w):
    rows = wt.shape[0] + out_w.shape[0]
    return pl.pallas_call(
        piece_kernel,
        out_shape=jax.ShapeDtypeStruct((rows, wt.shape[1] // 2), jnp.bfloat16),
        in_specs=[pl.BlockSpec(memory_space=pltpu.SMEM)] + any_specs(2),
        out_specs=pl.BlockSpec(memory_space=pltpu.VMEM),
        scratch_shapes=[pltpu.SemaphoreType.DMA((2,))],
        name="own_piece",
    )(core, wt, out_w)


def assemble_kernel(core_ref, *refs):
    sems = refs[-1]
    outs, parts = refs[-5:-1], refs[:-5]
    heads, hd, width = outs[0].shape
    cols = width // 2
    copies, head = [], 0
    for n, part in enumerate(parts):
        side = core_ref[0] if head < heads else 1 - core_ref[0]
        into_cols = pl.ds(pl.multiple_of(side * cols, cols), cols)
        count = part.shape[0]
        into_heads = pl.ds(head % heads, count)
        head += count
        for k, out in enumerate(outs):
            copies.append(
                pltpu.make_async_copy(
                    part.at[:, pl.ds(k * hd, hd)],
                    out.at[into_heads, :, into_cols],
                    sems.at[n * len(outs) + k],
                )
            )
    run_copies(copies)


def assemble(core, parts, heads, hd):
    cols = parts[0].shape[2]
    one = jax.ShapeDtypeStruct((heads, hd, 2 * cols), jnp.bfloat16)
    return pl.pallas_call(
        assemble_kernel,
        out_shape=(one,) * 4,
        in_specs=[pl.BlockSpec(memory_space=pltpu.SMEM)] + any_specs(len(parts)),
        out_specs=(pl.BlockSpec(memory_space=pltpu.VMEM),) * 4,
        scratch_shapes=[pltpu.SemaphoreType.DMA((4 * len(parts),))],
        name="assemble",
    )(core, *parts)


def tied(value, *others):
    return lax.optimization_barrier((value,) + others)[0]


def swap(value, bits, devices):
    return lax.ppermute(value, ("ctx", "head"), [(i, i ^ bits) for i in range(devices)])


def exchange_plan(pairs_dev, pairs_off, ctx_count, ctx_index, lower):
    pair_count = lower.shape[0]
    all_dev = pairs_dev.reshape(ctx_count, pair_count)
    all_off = pairs_off.reshape(ctx_count, pair_count)
    own = all_dev == ctx_index
    rank = jnp.sum((own[:, None, :] & lower[None]).astype(jnp.int32), axis=2)
    slot = jnp.arange(CAP, dtype=jnp.int32)
    chosen = own[:, None, :] & (rank[:, None, :] == slot[None, :, None])
    send = jnp.sum(jnp.where(chosen, all_off[:, None, :], 0), axis=2)
    send = send.reshape(-1)
    own_dev = lax.dynamic_index_in_dim(all_dev, ctx_index, 0, keepdims=False)
    earlier = (own_dev[:, None] == own_dev[None, :]) & lower
    take = own_dev * CAP + jnp.sum(earlier.astype(jnp.int32), axis=1)
    return send, take


def window_mask(lengths, first_pos, doc_tokens, rows):
    line_end = jnp.cumsum(lengths)
    positions = first_pos - BLK + jnp.arange(rows + 2 * BLK, dtype=jnp.int32)
    line = jnp.sum((line_end[None, :] <= positions[:, None]).astype(jnp.int32), axis=1)
    inside = (positions >= 0) & (positions < doc_tokens)
    line = jnp.where(inside, line, -1)
    masks = []
    for b in range(rows // BLK):
        keys = line[b * BLK : (b + 3) * BLK]
        queries = line[(b + 1) * BLK : (b + 2) * BLK]
        masks.append(jnp.where(keys[:, None] == queries[None, :], 0.0, NEG))
    return jnp.stack(masks).astype(jnp.float32)


def per_device(
    tokens, ln_gain, ln_bias, qkv_weight, out_weight, out_bias, lengths, pairs_dev, pairs_off
):
    ctx_count = lax.axis_size("ctx")
    heads = lax.axis_size("head")
    devices = ctx_count * heads
    ctx_index = lax.axis_index("ctx")
    head_index = lax.axis_index("head")
    rows, width = tokens.shape
    hd = width // heads

    wt = jnp.transpose(qkv_weight[:, 0, :])
    core = (ctx_index % 2).astype(jnp.int32).reshape(1)
    place = ctx_index * heads + head_index

    normed_t, first, last = layer_norm(tokens, ln_gain, ln_bias, heads)
    cells = lax.all_to_all(normed_t, "head", split_axis=0, concat_axis=0, tiled=True)

    own = own_piece(core, wt, out_weight)
    along_y = [list(range(first_x, heads, 2)) for first_x in range(2)]
    column = lax.all_gather(own, "head", axis_index_groups=along_y)

    both = ("ctx", "head")
    right = [(i, i + 1) for i in range(devices - 1)]
    left = [(i + 1, i) for i in range(devices - 1)]
    before = lax.ppermute(tied(last, cells), both, right)
    after = lax.ppermute(tied(first, cells), both, left)

    pair_count = (heads * rows // BLK) * RAND
    order = jnp.arange(pair_count, dtype=jnp.int32)
    lower = order[None, :] < order[:, None]
    send, take = exchange_plan(pairs_dev, pairs_off, ctx_count, ctx_index, lower)
    outgoing = pick_blocks(tied(send, own), cells)
    outgoing = outgoing.reshape(ctx_count, CAP * hd, BLK)
    slots = lax.all_to_all(outgoing, "ctx", split_axis=0, concat_axis=0, tiled=True)
    slots = slots.reshape(ctx_count * CAP, hd, BLK)

    half = column.shape[0] // 2
    mine = [column, swap(column[:half], 1, devices), swap(column[half:], 2 * heads + 1, devices)]
    other = [swap(part, heads, devices) for part in mine]
    shared = jnp.where(ctx_index == 0, cells[0, :, :BLK], 0).astype(jnp.bfloat16)
    group = 4
    for reach in (1, 2):
        hop = [(i, i + reach) for i in range(reach)]
        shared = shared + lax.ppermute(shared, "ctx", hop)
    copies = [
        lax.ppermute(shared, "ctx", [(i, i + reach) for i in range(group)])
        for reach in range(group, ctx_count, group)
    ]
    for copy in copies:
        shared = shared + copy
    placed = place_blocks(tied(take, column, before, after), slots, shared, heads)
    far = lax.all_to_all(placed, "head", split_axis=0, concat_axis=0, tiled=True)
    far = far.reshape(width, far.shape[2])

    near = jnp.concatenate([before, normed_t, after], axis=2)
    near = near.reshape(width, near.shape[2])

    mask = window_mask(lengths, place * rows, devices * rows, rows)

    f32 = jnp.float32
    bf16 = jnp.bfloat16
    weights = assemble(core, mine + other, heads, hd)
    w_q, w_k, w_v, w_o = (w.reshape(width, width) for w in weights)
    own_t = normed_t.reshape(width, rows)
    qt = jnp.dot(w_q, own_t, preferred_element_type=f32).astype(bf16)
    qt = (qt.astype(f32) * hd**-0.5).astype(bf16)
    k_near = lax.dot_general(near, w_k, TN, preferred_element_type=f32).astype(bf16)
    vt_near = jnp.dot(w_v, near, preferred_element_type=f32).astype(bf16)
    parts = near_attention(qt, k_near, vt_near, mask)
    attended = far_attention(qt, w_k, w_v, far, parts)
    projected = lax.dot_general(
        attended, w_o, (((0,), (0,)), ((), ())), preferred_element_type=f32
    )
    return (projected + out_bias).astype(bf16)


def solution(mesh):
    in_specs = (
        P(("ctx", "head"), None),
        P(),
        P(),
        P(None, "head", None),
        P("head", None),
        P(),
        P(),
        P(),
        P(),
    )

    return jax.shard_map(
        per_device,
        mesh=mesh,
        in_specs=in_specs,
        out_specs=P(("ctx", "head"), None),
        check_vma=False,
    )
```
